256 devices in a mesh: src: 32 (over z, y), rcv: 8 (over x, core).
Axes of the slice: x: 4, y: 4, z: 8, core: 2. Of those that a mesh axis runs over, the one named last changes fastest.
Arguments:
- field: bfloat16 [2, 16384, 4096], P(None, 'rcv', 'src'), may hold values from -6 to 6
- u_basis: bfloat16 [32, 8, 2, 8, 2, 160, 256], P('src', 'rcv'), may hold values from -0.0390625 to 0.0390625
- v_basis: bfloat16 [32, 8, 2, 8, 160, 2, 256], P('src', 'rcv'), may hold values from -0.25 to 0.25
- tile_ranks: int32 [32, 8, 2, 8], P('src', 'rcv'), may hold values from 32 to 160, as said below
- window_start: int32 [32], replicated, may hold values from 0 to 56
Outputs:
- predicted: bfloat16 [2, 2048, 4096], P(None, 'rcv', 'src')
The draws below stay inside these ranges and needn't reach their ends.
Inputs may be any that keep to these rules, and one draw needn't show every extreme that they name: `tile_ranks`: on every device of the mesh at least one of its tiles has rank 160.
All inputs are finite; a program needn't handle non-finite values.
Results may differ from the reference program's by a relative error of at most 0.0058.
Values may be sent and summed in bfloat16 or wider, within the bound.
A program may use at most 192 MiB of HBM per device.

```python
import jax
import jax.numpy as jnp
from jax import lax

B = 256
RMAX = 160
RMIN = 32
JT = 8
MTD = 2
AR = 8
CD = 128
NT = 64
MT = 64
N = 16384
C = 4096
N_SRC = 32
N_RCV = 8


def draw_tile_ranks(key, part):
    first_key, second_key = jax.random.split(jax.random.fold_in(key, 17))
    base_ranks = jax.random.randint(first_key, (N_SRC, N_RCV, MTD * JT), RMIN, RMAX + 1, dtype=jnp.int32)
    chosen_spot = jax.random.randint(second_key, (N_SRC, N_RCV), 0, MTD * JT, dtype=jnp.int32)
    spot_hit = jnp.arange(MTD * JT, dtype=jnp.int32)[None, None, :] == chosen_spot[:, :, None]
    full_ranks = jnp.where(spot_hit, jnp.int32(RMAX), base_ranks)
    return full_ranks.reshape(N_SRC, N_RCV, MTD, JT)


def with_ends(values, stream_key, low, largest):
    place = [jax.random.randint(jax.random.fold_in(stream_key, axis), (), 0, length) for axis, length in enumerate(values.shape)]
    main_axis = values.shape.index(max(values.shape))
    beside = place[:main_axis] + [(place[main_axis] + 1) % values.shape[main_axis]] + place[main_axis + 1:]
    return values.at[tuple(place)].set(low).at[tuple(beside)].set(largest)


def block_scale(own_key, extent, pieces, smallest, high):
    loudness = 1.0
    for dim, parts in pieces:
        steps = jax.random.uniform(jax.random.fold_in(jax.random.fold_in(own_key, 6), dim), (parts,), jnp.float32, smallest / len(pieces), high / len(pieces))
        loudness = loudness * jnp.repeat(jnp.exp(steps), extent[dim] // parts).reshape((-1,) + (1,) * (len(extent) - 1 - dim))
    return loudness


def gaussian(key, dims, width, reach, cuts=(), kind=jnp.bfloat16):
    result = width * jax.random.normal(key, dims, jnp.float32)
    if cuts:
        result = result * block_scale(key, dims, cuts, -0.22, 0.18)
    return jnp.clip(result, -reach, reach).astype(kind)


def setup_inputs(seed: int = 0) -> dict:
    streams_of = jax.random.split(jax.random.key(seed), 6)
    return {
        "field": gaussian(streams_of[0], (2, N, C), 1.0, 6.0, ((1, 8), (2, 32))),
        "u_basis": gaussian(streams_of[1], (N_SRC, N_RCV, MTD, JT, 2, RMAX, B), (2 * RMAX * NT) ** -0.5, 0.0390625, ((0, 32), (1, 8))),
        "v_basis": gaussian(streams_of[2], (N_SRC, N_RCV, MTD, JT, RMAX, 2, B), (2 * B) ** -0.5, 0.25, ((0, 32), (1, 8))),
        "tile_ranks": draw_tile_ranks(jax.random.fold_in(streams_of[5], 71), 0),
        "window_start": with_ends(jax.random.randint(streams_of[4], (N_SRC,), 0, MT - AR + 1), jax.random.fold_in(streams_of[4], 1), 0, MT - AR).astype(jnp.int32),
    }


def expand_block(field_block):
    real_part = field_block[0]
    imag_part = field_block[1]
    upper = jnp.concatenate([real_part, imag_part], axis=1)
    lower = jnp.concatenate([imag_part, -real_part], axis=1)
    return jnp.concatenate([upper, lower], axis=0)


def tile_products(u_tiles, v_tiles, rank_list, expanded):
    n_items = v_tiles.shape[0]
    rank_most = v_tiles.shape[1]
    flat_v = v_tiles.reshape(n_items, rank_most, -1).astype(jnp.float32)
    projected = jnp.einsum('nkq,qc->nkc', flat_v, expanded.astype(jnp.float32))
    rank_keep = jnp.arange(rank_most, dtype=jnp.int32)[None, :] < rank_list[:, None]
    projected = jnp.where(rank_keep[:, :, None], projected, jnp.float32(0.0)).astype(jnp.bfloat16)
    half_cols = projected.shape[2] // 2
    w_real = projected[:, :, :half_cols]
    w_imag = projected[:, :, half_cols:]
    stacked = jnp.concatenate([projected, jnp.concatenate([-w_imag, w_real], axis=2)], axis=1)
    flat_u = u_tiles.reshape(n_items, 2 * rank_most, -1).astype(jnp.float32)
    return jnp.einsum('nkp,nkc->npc', flat_u, stacked.astype(jnp.float32))


def reference(field, u_basis, v_basis, tile_ranks, window_start):
    spacing = N_SRC // JT
    steps_t = jnp.arange(AR, dtype=jnp.int32)

    def one_reader(reader):
        first_row = window_start[reader]
        row_ids = first_row + steps_t
        columns = lax.dynamic_slice_in_dim(field, reader * CD, CD, 2)

        def add_column(running, col):
            col_group = col // JT
            col_local = col % JT
            field_block = lax.dynamic_slice_in_dim(columns, col * B, B, 1)
            expanded = expand_block(field_block)
            owners = ((row_ids + spacing * col_local) % N_SRC).astype(jnp.int32)
            levels = (row_ids // N_SRC).astype(jnp.int32)
            u_tiles = u_basis[owners, col_group, levels, col_local]
            v_tiles = v_basis[owners, col_group, levels, col_local]
            rank_list = tile_ranks[owners, col_group, levels, col_local]
            term = tile_products(u_tiles, v_tiles, rank_list, expanded).astype(jnp.bfloat16)
            term = lax.optimization_barrier(term)
            return running + term.astype(jnp.float32), None

        start_sum = jnp.zeros((AR, B, 2 * CD), jnp.float32)
        running, unused = lax.scan(add_column, start_sum, jnp.arange(NT, dtype=jnp.int32))
        return running

    reader_parts = lax.map(one_reader, jnp.arange(N_SRC, dtype=jnp.int32))
    arranged = reader_parts.reshape(N_SRC, AR * B, 2, CD).transpose(2, 1, 0, 3)
    return arranged.reshape(2, AR * B, N_SRC * CD).astype(jnp.bfloat16)
```

```python
import jax
import jax.numpy as jnp
from jax import lax
from jax.experimental import pallas as pl
from jax.experimental.pallas import tpu as pltpu
from jax.sharding import PartitionSpec as P

MESH = pl.DeviceIdType.MESH
BF = jnp.bfloat16
F32 = jnp.float32
NZ, NY, NX = 8, 4, 4
STEPS = 8


def rem(a, b):
    return lax.rem(a, jnp.int32(b))


def div(a, b):
    return lax.div(a, jnp.int32(b))


def kernel(
    field_ref, u_ref, v_ref, rank_ref, ws_ref, out_ref,
    fbuf, gx, zb, mids, oths, osend, relay, terms, crecv, xs, xr, zsb, zr, fin, fr,
    uraw, vraw, ut, v2,
    lsem, zss, zrs, yss, yrs, css, crs, xss, xrs, gss, grs, fss, frs,
):
    src = lax.axis_index("src")
    rcv = lax.axis_index("rcv")
    z, y = div(src, NY), rem(src, NY)
    x, core = div(rcv, 2), rem(rcv, 2)

    def zdev(offset):
        return (rem(z + (offset + 2 * NZ), NZ) * NY + y, rcv)

    def ydev(offset):
        return (z * NY + rem(y + (offset + NY), NY), rcv)

    sibling = (src, x * 2 + 1 - core)

    def rcopy(source, target, ss, rs, device):
        return pltpu.make_async_remote_copy(
            src_ref=source, dst_ref=target, send_sem=ss, recv_sem=rs,
            device_id=device, device_id_type=MESH,
        )

    load_f = pltpu.make_async_copy(field_ref, fbuf, lsem.at[0])
    load_v = pltpu.make_async_copy(v_ref, vraw, lsem.at[1])
    load_u = pltpu.make_async_copy(u_ref, uraw, lsem.at[2])
    load_f.start()
    load_v.start()
    load_u.start()

    barrier = pltpu.get_barrier_semaphore()
    for offset in range(1, NZ):
        pl.semaphore_signal(barrier, inc=1, device_id=zdev(offset), device_id_type=MESH)
    for offset in range(1, NY):
        pl.semaphore_signal(barrier, inc=1, device_id=ydev(offset), device_id_type=MESH)
    pl.semaphore_signal(barrier, inc=1, device_id=sibling, device_id_type=MESH)
    for offset in range(1, NX):
        pl.semaphore_signal(
            barrier, inc=1, device_id=(src, rem(x + offset, NX) * 2 + core), device_id_type=MESH
        )
    for k in range(4):
        t_src, t_rcv = z * NY + x, core * 4 + k

        @pl.when(jnp.logical_or(t_src != src, t_rcv != rcv))
        def _():
            pl.semaphore_signal(barrier, inc=1, device_id=(t_src, t_rcv), device_id_type=MESH)

        s_src, s_rcv = z * NY + k, y * 2 + div(x, 2)

        @pl.when(jnp.logical_or(s_src != src, s_rcv != rcv))
        def _():
            pl.semaphore_signal(barrier, inc=1, device_id=(s_src, s_rcv), device_id_type=MESH)

    own_final = jnp.where(jnp.logical_and(x == y, div(x, 2) == core), 1, 0).astype(jnp.int32)

    load_f.wait()
    shift = z + 19 - lax.shift_right_logical(ws_ref[src], jnp.int32(2))

    def roll_block(j, carry):
        block = lax.bitwise_and(shift + j, jnp.int32(7))
        gx[j, :, 0:128] = fbuf[0, block]
        gx[j, :, 128:256] = fbuf[1, block]
        return carry

    lax.fori_loop(0, 10, roll_block, 0)
    pl.semaphore_wait(barrier, 14 + 8 - 2 * own_final)

    def plane(m):
        h = div(m + 1, 2)
        odd = rem(m, 2)
        return rem(z + 8 + h - 2 * h * odd, NZ)

    def zcopy(source, m, kk, direction):
        return rcopy(source, zb.at[m - 1, kk], zss.at[m - 1, kk], zrs.at[m - 1, kk], zdev(direction))

    def ycopy(m, i, mid=None):
        toward = ydev(-1) if i in (3, 4, 5, 8, 9) else ydev(1)
        top, low = pl.ds(0, 128), pl.ds(128, 128)
        if i in (0, 3):
            source, target = (mids.at[m, 0] if mid is None else mid), mids.at[m, 3 if i == 0 else 1]
        elif i == 1:
            source, target = osend.at[m, 0], oths.at[m, 3]
        elif i == 2:
            source, target = osend.at[m, 2, top], relay.at[m, 0]
        elif i == 4:
            source, target = osend.at[m, 1], oths.at[m, 1]
        elif i == 5:
            source, target = osend.at[m, 2, low], relay.at[m, 1]
        elif i == 6:
            source, target = mids.at[m, 3, top], mids.at[m, 2, top]
        elif i == 7:
            source, target = relay.at[m, 0], oths.at[m, 2, top]
        elif i == 8:
            source, target = mids.at[m, 1, low], mids.at[m, 2, low]
        else:
            source, target = relay.at[m, 1], oths.at[m, 2, low]
        return rcopy(source, target, yss.at[m, i], yrs.at[m, i], toward)

    def ysend(m, mid, upper, lower):
        reader = plane(m) * NY + y
        phase = lax.bitwise_and(ws_ref[reader], jnp.int32(3))

        def rows(i, carry):
            at = pl.ds(pl.multiple_of(i * 32, 32), 32)
            mids[m, 0, at] = mid[at]
            one, two = upper[at], lower[at]
            for k, target in enumerate((oths.at[m, 0], osend.at[m, 0], osend.at[m, 1], osend.at[m, 2])):
                side = rem(y + (0, 1, 3, 2)[k], NY)
                target[at] = jnp.where(side >= phase, one, two)
            return carry

        lax.fori_loop(0, 8, rows, 0)
        for i in (0, 3, 2, 5, 1, 4):
            ycopy(m, i, mid).start()

    def yrelay(m):
        for came, onward in ((0, 6), (3, 8), (2, 7), (5, 9)):
            ycopy(m, came).wait_recv()
            ycopy(m, onward).start()

    def zneeded(m):
        h = div(m + 1, 2)

        @pl.when(rem(m, 2) == 1)
        def _():
            for i in range(3):
                kk = h - 1 + i
                zcopy(zb.at[m - 1, kk], m, kk, 1).wait_recv()
                if i > 0:
                    @pl.when(h < 4)
                    def _():
                        zcopy(zb.at[m - 1, kk], m + 2, kk, 1).start()
            ysend(m, zb.at[m - 1, h], zb.at[m - 1, h + 1], zb.at[m - 1, h - 1])

        @pl.when(rem(m, 2) == 0)
        def _():
            for i in range(3):
                kk = 5 - h - i
                zcopy(zb.at[m - 1, kk], m, kk, -1).wait_recv()
                if i > 0:
                    @pl.when(h < 3)
                    def _():
                        zcopy(zb.at[m - 1, kk], m + 2, kk, -1).start()
            ysend(m, zb.at[m - 1, 4 - h], zb.at[m - 1, 5 - h], zb.at[m - 1, 3 - h])

    def zrest(m):
        h = div(m + 1, 2)

        @pl.when(rem(m, 2) == 1)
        def _():
            def go(kk, carry):
                zcopy(zb.at[m - 1, kk], m, kk, 1).wait_recv()
                zcopy(zb.at[m - 1, kk], m + 2, kk, 1).start()
                return carry

            lax.fori_loop(h + 2, 6, go, 0)

        @pl.when(rem(m, 2) == 0)
        def _():
            def go(i, carry):
                kk = 2 - h - i
                zcopy(zb.at[m - 1, kk], m, kk, -1).wait_recv()
                zcopy(zb.at[m - 1, kk], m + 2, kk, -1).start()
                return carry

            lax.fori_loop(0, 3 - h, go, 0)

    def ccopy(m, k):
        return rcopy(terms.at[0, m, k], crecv.at[m, k], css.at[m, k], crs.at[m, k], sibling)

    def compute(m):
        first = plane(m) * NY

        def unit(i, carry):
            k = i + jnp.where(i == 2, 1, 0) - jnp.where(i == 3, 1, 0)
            @pl.when(k == 1)
            def _():
                ycopy(m, 4).wait_recv()

            @pl.when(k == 3)
            def _():
                ycopy(m, 1).wait_recv()

            @pl.when(k == 2)
            def _():
                for j in range(6, 10):
                    ycopy(m, j).wait_recv()

            start = ws_ref[first + rem(y + k, NY)]
            phase = lax.bitwise_and(start, jnp.int32(3))
            late = jnp.where(y < phase, 1, 0).astype(jnp.int32)
            group = lax.shift_right_logical(start, jnp.int32(2)) + late
            column = lax.bitwise_and(z + 16 - group, jnp.int32(7))
            row = group * 4 + y
            tile0 = lax.shift_right_logical(row, jnp.int32(5)) * 8 + column
            tile1 = lax.shift_right_logical(row + 4, jnp.int32(5)) * 8 + lax.bitwise_and(column + 7, jnp.int32(7))

            def item(w, inner):
                e = rem(core + 1 + w, 2)
                tile = jnp.where(e == 0, tile0, tile1)
                block = jnp.where(e + late == 1, mids[m, k], oths[m, k])
                parts = jnp.dot(v2[tile], block, preferred_element_type=F32)
                w_real = (parts[:160, :128] + parts[160:, 128:]).astype(BF)
                w_imag = (parts[:160, 128:] - parts[160:, :128]).astype(BF)
                stacked = jnp.concatenate(
                    [
                        jnp.concatenate([w_real, w_imag], axis=1),
                        jnp.concatenate([-w_imag, w_real], axis=1),
                    ],
                    axis=0,
                )
                terms[w, m, k] = jnp.dot(ut[tile], stacked, preferred_element_type=F32).astype(BF)
                return inner

            lax.fori_loop(0, 2, item, 0)
            ccopy(m, k).start()
            return carry

        lax.fori_loop(0, 4, unit, 0)

    def xcopy(m, k):
        owner = rem(y + k, NY)
        slot = rem(x + NX - owner, NX) - 1
        return rcopy(xs.at[m, k], xr.at[m, slot], xss.at[m, k], xrs.at[m, slot], (src, owner * 2 + core))

    def core_sum(m):
        def unit(k, carry):
            ccopy(m, k).wait_recv()
            xs[m, k] = (terms[1, m, k].astype(F32) + crecv[m, k].astype(F32)).astype(BF)
            return carry

        lax.fori_loop(0, 4, unit, 0)

        def send(k, carry):
            @pl.when(rem(y + k, NY) != x)
            def _():
                xcopy(m, k).start()

            return carry

        lax.fori_loop(0, 4, send, 0)

    def gcopy(m):
        return rcopy(zsb.at[m], zr.at[m], gss.at[m], grs.at[m], (plane(m) * NY + y, rcv))

    def x_sum(m):
        for j in range(3):
            rcopy(xr.at[m, j], xr.at[m, j], xss.at[m, 0], xrs.at[m, j], sibling).wait_recv()
        total = xs[m, rem(x + NY - y, NY)].astype(F32)
        for j in range(3):
            total = total + xr[m, j].astype(F32)
        zsb[m] = total.astype(BF)

        @pl.when(m > 0)
        def _():
            gcopy(m).start()

    for i in range(6):
        zcopy(gx.at[i + 4], 1, i, 1).start()
        if i < 5:
            zcopy(gx.at[4 - i], 2, 4 - i, -1).start()
    ysend(jnp.int32(0), gx.at[4], gx.at[5], gx.at[3])

    load_v.wait()
    load_u.wait()

    def prepare(t, carry):
        keep = lax.broadcasted_iota(jnp.int32, (160, 256), 0) < rank_ref[t]
        for c in range(2):
            part = vraw[t, :, c, :]
            v2[t, c * 160:(c + 1) * 160, :] = jnp.where(keep, part, jnp.zeros_like(part))
        ut[t] = jnp.transpose(uraw[t])
        return carry

    lax.fori_loop(0, 16, prepare, 0)
    yrelay(jnp.int32(0))
    zneeded(jnp.int32(1))

    def step(n, carry):
        @pl.when(n < 7)
        def _():
            yrelay(n + 1)

        @pl.when(n < 6)
        def _():
            zneeded(n + 2)

        @pl.when(n < 8)
        def _():
            compute(n)

        @pl.when(n == 0)
        def _():
            zrest(n + 1)

        @pl.when(n < 5)
        def _():
            zrest(n + 2)

        @pl.when(jnp.logical_and(n > 0, n < 9))
        def _():
            core_sum(n - 1)

        @pl.when(n > 1)
        def _():
            x_sum(n - 2)

        return carry

    lax.fori_loop(0, STEPS + 2, step, 0)

    total = zsb[0].astype(F32)
    for m in range(1, STEPS):
        gcopy(jnp.int32(m)).wait_recv()
        total = total + zr[m].astype(F32)
    fin[...] = total.astype(BF)

    def fcopy(k):
        return rcopy(fin, fr.at[y], fss.at[k], frs.at[y], (z * NY + x, core * 4 + k))

    def mine(k):
        return jnp.logical_and(x == y, core * 4 + k == rcv)

    for k in range(4):
        @pl.when(jnp.logical_not(mine(k)))
        def _():
            fcopy(k).start()

        @pl.when(mine(k))
        def _():
            fr[y] = fin[...]

    for k in range(4):
        @pl.when(jnp.logical_or(y != k, own_final == 0))
        def _():
            rcopy(fin, fr.at[k], fss.at[k], frs.at[k], sibling).wait_recv()

    turn = lax.bitwise_and(rem(rcv, 4) + ws_ref[src], jnp.int32(3))
    result = fr[turn]
    out_ref[0] = result[:, 0:128]
    out_ref[1] = result[:, 128:256]

    for k in range(4):
        @pl.when(jnp.logical_not(mine(k)))
        def _():
            fcopy(k).wait_send()

    for i in range(6):
        zcopy(gx.at[i + 4], 1, i, 1).wait_send()
        if i < 5:
            zcopy(gx.at[4 - i], 2, 4 - i, -1).wait_send()

    def drain(m, carry):
        for i in range(10):
            ycopy(m, i).wait_send()

        def inner(k, c):
            ccopy(m, k).wait_send()

            @pl.when(rem(y + k, NY) != x)
            def _():
                xcopy(m, k).wait_send()

            return c

        lax.fori_loop(0, 4, inner, 0)

        @pl.when(m > 0)
        def _():
            gcopy(m).wait_send()

        h = div(m + 1, 2)

        @pl.when(jnp.logical_and(rem(m, 2) == 1, h > 1))
        def _():
            def go(kk, c):
                zcopy(zb.at[0, kk], m, kk, 1).wait_send()
                return c

            lax.fori_loop(h - 1, 6, go, 0)

        @pl.when(jnp.logical_and(rem(m, 2) == 0, h > 1))
        def _():
            def go(kk, c):
                zcopy(zb.at[0, kk], m, kk, -1).wait_send()
                return c

            lax.fori_loop(0, 6 - h, go, 0)

        return carry

    lax.fori_loop(0, STEPS, drain, 0)


def body(field, u_basis, v_basis, tile_ranks, window_start):
    fields = field.reshape(2, 8, 256, 128)
    u_tiles = u_basis.reshape(16, 320, 256)
    v_tiles = v_basis.reshape(16, 160, 2, 256)
    ranks = tile_ranks.reshape(16)

    def blocks(*lead):
        return pltpu.VMEM((*lead, 256, 256), BF)

    def sems(*shape):
        return pltpu.SemaphoreType.DMA(shape)

    anywhere = pl.BlockSpec(memory_space=pl.ANY)
    scalars = pl.BlockSpec(memory_space=pltpu.SMEM)
    return pl.pallas_call(
        kernel,
        out_shape=jax.ShapeDtypeStruct((2, 256, 128), BF),
        in_specs=[anywhere, anywhere, anywhere, scalars, scalars],
        out_specs=pl.BlockSpec(memory_space=pltpu.VMEM),
        scratch_shapes=[
            pltpu.VMEM((2, 8, 256, 128), BF),
            blocks(10), blocks(7, 6), blocks(8, 4), blocks(8, 4), blocks(8, 3),
            pltpu.VMEM((8, 2, 128, 256), BF),
            blocks(2, 8, 4), blocks(8, 4), blocks(8, 4), blocks(8, 3), blocks(8), blocks(8),
            blocks(), blocks(4),
            pltpu.VMEM((16, 320, 256), BF),
            pltpu.VMEM((16, 160, 2, 256), BF),
            pltpu.VMEM((16, 256, 320), BF),
            pltpu.VMEM((16, 320, 256), BF),
            sems(3), sems(7, 6), sems(7, 6), sems(8, 10), sems(8, 10), sems(8, 4), sems(8, 4),
            sems(8, 4), sems(8, 3), sems(8), sems(8), sems(4), sems(4),
        ],
        compiler_params=pltpu.CompilerParams(
            collective_id=0, has_side_effects=True, vmem_limit_bytes=60 * 1024 * 1024
        ),
    )(fields, u_tiles, v_tiles, ranks, window_start)


def solution(mesh):
    return jax.shard_map(
        body,
        mesh=mesh,
        in_specs=(
            P(None, "rcv", "src"),
            P("src", "rcv", None, None, None, None, None),
            P("src", "rcv", None, None, None, None, None),
            P("src", "rcv", None, None),
            P(),
        ),
        out_specs=P(None, "rcv", "src"),
        check_vma=False,
    )
```

```python
import jax
import jax.numpy as jnp
from jax import lax
from jax.experimental import pallas as pl
from jax.experimental.pallas import tpu as pltpu
from jax.sharding import PartitionSpec as P

MESH = pl.DeviceIdType.MESH
BF = jnp.bfloat16
F32 = jnp.float32
NZ, NY, NX = 8, 4, 4
STEPS = 8


def rem(a, b):
    return lax.rem(a, jnp.int32(b))


def div(a, b):
    return lax.div(a, jnp.int32(b))


def kernel(
    field_ref, u_ref, v_ref, rank_ref, ws_ref, out_ref,
    fbuf, gx, zb, mids, oths, osend, relay, fsend, terms, crecv, xs, xr, zsb, zr, fin, fr, fsw, fso,
    uraw, vraw, ut, v2,
    lsem, zss, zrs, yss, yrs, wss, wrs, css, crs, xss, xrs, gss, grs, fss, frs, sss, srs,
):
    src = lax.axis_index("src")
    rcv = lax.axis_index("rcv")
    z, y = div(src, NY), rem(src, NY)
    x, core = div(rcv, 2), rem(rcv, 2)
    own_y, own_e = rem(x, 2) * 2 + core, div(x, 2)
    at_home = own_y == y
    home = jnp.where(at_home, 1, 0).astype(jnp.int32)

    def zdev(offset):
        return (rem(z + (offset + 2 * NZ), NZ) * NY + y, rcv)

    def ydev(offset):
        return (z * NY + rem(y + (offset + NY), NY), rcv)

    sibling = (src, x * 2 + 1 - core)

    def rcopy(source, target, ss, rs, device):
        return pltpu.make_async_remote_copy(
            src_ref=source, dst_ref=target, send_sem=ss, recv_sem=rs,
            device_id=device, device_id_type=MESH,
        )

    load_f = pltpu.make_async_copy(field_ref, fbuf, lsem.at[0])
    load_v = pltpu.make_async_copy(v_ref, vraw, lsem.at[1])
    load_u = pltpu.make_async_copy(u_ref, uraw, lsem.at[2])
    load_f.start()

    barrier = pltpu.get_barrier_semaphore()

    def greet(device):
        pl.semaphore_signal(barrier, inc=1, device_id=device, device_id_type=MESH)

    for offset in (4, 3, 5, 2, 6, 1, 7):
        greet(zdev(offset))
    for offset in range(1, NY):
        greet(ydev(offset))
    greet(sibling)
    for offset in range(1, NX):
        greet((src, rem(x + offset, NX) * 2 + core))

    def last_target(j):
        return (z * NY + own_y, (own_e * 2 + j) * 2 + rem(y, 2))

    def stays(j):
        return jnp.logical_and(at_home, rem(x, 2) == j)

    for j in range(2):
        @pl.when(jnp.logical_not(stays(j)))
        def _():
            greet(last_target(j))

        @pl.when(jnp.logical_not(jnp.logical_and(at_home, div(y, 2) == j)))
        def _():
            greet((z * NY + core + 2 * j, (own_e * 2 + div(y, 2)) * 2 + rem(y, 2)))

    load_f.wait()
    load_v.start()
    load_u.start()
    shift = z + 19 - lax.shift_right_logical(ws_ref[src], jnp.int32(2))

    def roll_block(j, carry):
        block = lax.bitwise_and(shift + j, jnp.int32(7))
        gx[j, :, 0:128] = fbuf[0, block]
        gx[j, :, 128:256] = fbuf[1, block]
        return carry

    lax.fori_loop(0, 10, roll_block, 0)
    pl.semaphore_wait(barrier, 14 + 4 - 2 * home)

    def hop(m):
        return div(m + 1, 2) + jnp.where(m == 6, 1, 0) - jnp.where(m == 7, 1, 0)

    def plus(m):
        return rem(m + jnp.where(m > 5, 1, 0), 2) == 1

    def plane(m):
        h = hop(m)
        return rem(z + 8 + jnp.where(plus(m), -h, h), NZ)

    def forwarded(m):
        return jnp.logical_or(m == 4, m == 7)

    def zcopy(source, chain, kk, direction):
        return rcopy(source, zb.at[chain, kk], zss.at[chain, kk], zrs.at[chain, kk], zdev(direction))

    def ycopy(m, i, mid=None, thin=False):
        toward = ydev(-1) if i in (3, 4, 5, 8, 9) else ydev(1)
        top, low = pl.ds(0, 128), pl.ds(128, 128)
        other = mids if thin else oths
        if i in (0, 3):
            source, target = (mids.at[m, 0] if mid is None else mid), mids.at[m, 3 if i == 0 else 1]
        elif i == 1:
            source, target = osend.at[m, 0], other.at[m, 3]
        elif i == 2:
            source, target = osend.at[m, 2, top], relay.at[m, 0]
        elif i == 4:
            source, target = osend.at[m, 1], other.at[m, 1]
        elif i == 5:
            source, target = osend.at[m, 2, low], relay.at[m, 1]
        elif i == 6:
            source, target = mids.at[m, 3, top], mids.at[m, 2, top]
        elif i == 7:
            source, target = relay.at[m, 0], other.at[m, 2, top]
        elif i == 8:
            source, target = mids.at[m, 1, low], mids.at[m, 2, low]
        else:
            source, target = relay.at[m, 1], other.at[m, 2, low]
        return rcopy(source, target, yss.at[m, i], yrs.at[m, i], toward)

    sides = (0, 1, 3, 2)

    def phase_of(m):
        return lax.bitwise_and(ws_ref[plane(m) * NY + y], jnp.int32(3))

    def ysend(m, mid, upper, lower):
        phase = phase_of(m)

        def rows(i, carry):
            at = pl.ds(pl.multiple_of(i * 32, 32), 32)
            mids[m, 0, at] = mid[at]
            one, two = upper[at], lower[at]
            for k, target in enumerate((oths.at[m, 0], osend.at[m, 0], osend.at[m, 1], osend.at[m, 2])):
                target[at] = jnp.where(rem(y + sides[k], NY) >= phase, one, two)
            return carry

        lax.fori_loop(0, 8, rows, 0)
        for i in (0, 3, 2, 5, 1, 4):
            ycopy(m, i, mid).start()

    def ysend_thin(m, mid, upper, lower):
        phase = phase_of(m)

        def rows(i, carry):
            at = pl.ds(pl.multiple_of(i * 32, 32), 32)
            one, two = mid[at], lower[at]
            oths[m, 0, at] = jnp.where(y >= phase, upper[at], one)
            for k, target in enumerate((mids.at[m, 0], osend.at[m, 0], osend.at[m, 1], osend.at[m, 2])):
                target[at] = jnp.where(rem(y + sides[k], NY) >= phase, one, two)
            return carry

        lax.fori_loop(0, 8, rows, 0)
        for i in (2, 5, 1, 4):
            ycopy(m, i, thin=True).start()

    def yrelay(m):
        @pl.when(jnp.logical_not(forwarded(m)))
        def _():
            for came, onward in ((0, 6), (3, 8), (2, 7), (5, 9)):
                if came in (0, 3):
                    @pl.when(m > 0)
                    def _():
                        ycopy(m, came).wait_recv()
                else:
                    ycopy(m, came).wait_recv()
                ycopy(m, onward).start()

        @pl.when(forwarded(m))
        def _():
            for came, onward in ((2, 7), (5, 9)):
                ycopy(m, came, thin=True).wait_recv()
                ycopy(m, onward, thin=True).start()

    def zneeded(m):
        h = hop(m)

        @pl.when(plus(m))
        def _():
            chain = h - 1
            for i in range(3):
                kk = h - 1 + i
                zcopy(zb.at[chain, kk], chain, kk, 1).wait_recv()
                if i > 0:
                    @pl.when(h < 4)
                    def _():
                        zcopy(zb.at[chain, kk], chain + 1, kk, 1).start()
            ysend(m, zb.at[chain, h], zb.at[chain, h + 1], zb.at[chain, h - 1])

        @pl.when(jnp.logical_not(plus(m)))
        def _():
            chain = h + 3
            for i in range(3):
                kk = 5 - h - i
                zcopy(zb.at[chain, kk], chain, kk, -1).wait_recv()
                if i > 0:
                    @pl.when(h < 3)
                    def _():
                        zcopy(zb.at[chain, kk], chain + 1, kk, -1).start()
            blocks = zb.at[chain, 4 - h], zb.at[chain, 5 - h], zb.at[chain, 3 - h]

            @pl.when(h == 1)
            def _():
                ysend(m, *blocks)

            @pl.when(h > 1)
            def _():
                ysend_thin(m, *blocks)

    def zrest(m):
        h = hop(m)

        @pl.when(plus(m))
        def _():
            def go(kk, carry):
                zcopy(zb.at[h - 1, kk], h - 1, kk, 1).wait_recv()
                zcopy(zb.at[h - 1, kk], h, kk, 1).start()
                return carry

            lax.fori_loop(h + 2, 6, go, 0)

        @pl.when(jnp.logical_not(plus(m)))
        def _():
            def go(i, carry):
                kk = 2 - h - i
                zcopy(zb.at[h + 3, kk], h + 3, kk, -1).wait_recv()
                zcopy(zb.at[h + 3, kk], h + 4, kk, -1).start()
                return carry

            lax.fori_loop(0, 3 - h, go, 0)

    def wcopy(k, late_step):
        if late_step:
            return rcopy(mids.at[4, k], oths.at[7, k], wss.at[1, k - 1], wrs.at[1, k - 1], zdev(-1))
        return rcopy(fsend.at[k - 1], oths.at[4, k], wss.at[0, k - 1], wrs.at[0, k - 1], zdev(-1))

    def mine(k):
        return rem(y + k, 2) == core

    def ccopy(m, k, e):
        j = div(k, 2)
        return rcopy(terms.at[m, k, e], crecv.at[m, j, e], css.at[m, j, e], crs.at[m, j, e], sibling)

    def product(m, k):
        fwd = forwarded(m)

        @pl.when(jnp.logical_and(k == 1, m == 0))
        def _():
            ycopy(m, 3).wait_recv()

        @pl.when(jnp.logical_and(k == 3, m == 0))
        def _():
            ycopy(m, 0).wait_recv()

        @pl.when(k == 1)
        def _():
            ycopy(m, 4).wait_recv()

        @pl.when(k == 3)
        def _():
            ycopy(m, 1).wait_recv()

        @pl.when(k == 2)
        def _():
            ycopy(m, 7).wait_recv()
            ycopy(m, 9).wait_recv()

        @pl.when(jnp.logical_and(k == 2, jnp.logical_not(fwd)))
        def _():
            ycopy(m, 6).wait_recv()
            ycopy(m, 8).wait_recv()

        @pl.when(jnp.logical_and(k > 0, m == 4))
        def _():
            wcopy(k, True).start()
            wcopy(k, False).wait_recv()

        @pl.when(jnp.logical_and(k > 0, m == 7))
        def _():
            wcopy(k, True).wait_recv()

        start = ws_ref[plane(m) * NY + rem(y + k, NY)]
        phase = lax.bitwise_and(start, jnp.int32(3))
        late = jnp.where(y < phase, 1, 0).astype(jnp.int32)
        group = lax.shift_right_logical(start, jnp.int32(2)) + late
        column = lax.bitwise_and(z + 16 - group, jnp.int32(7))
        row = group * 4 + y
        tile0 = lax.shift_right_logical(row, jnp.int32(5)) * 8 + column
        tile1 = lax.shift_right_logical(row + 4, jnp.int32(5)) * 8 + lax.bitwise_and(column + 7, jnp.int32(7))
        swap = jnp.where(fwd, 0, late)

        @pl.when(jnp.logical_and(k > 0, m == 2))
        def _():
            fsend[k - 1] = jnp.where(late == 0, mids[m, k], oths[m, k])

        def item(e, inner):
            tile = jnp.where(e == 0, tile0, tile1)
            block = jnp.where(e + swap == 1, mids[m, k], oths[m, k])
            parts = jnp.dot(v2[tile], block, preferred_element_type=F32)
            w_real = (parts[:160, :128] + parts[160:, 128:]).astype(BF)
            w_imag = (parts[:160, 128:] - parts[160:, :128]).astype(BF)
            stacked = jnp.concatenate(
                [
                    jnp.concatenate([w_real, w_imag], axis=1),
                    jnp.concatenate([-w_imag, w_real], axis=1),
                ],
                axis=0,
            )
            terms[m, k, e] = jnp.dot(ut[tile], stacked, preferred_element_type=F32).astype(BF)
            return inner

        lax.fori_loop(0, 2, item, 0)

        @pl.when(jnp.logical_not(mine(k)))
        def _():
            ccopy(m, k, 0).start()
            ccopy(m, k, 1).start()

        @pl.when(jnp.logical_and(k > 0, m == 2))
        def _():
            wcopy(k, False).start()

    def xcopy(m, k, e):
        j = div(k, 2)
        owner = 2 * e + div(rem(y + k, NY), 2)
        slot = lax.max(rem(x + NX - owner, NX) - 1, jnp.int32(0))
        return rcopy(
            xs.at[m, j, e], xr.at[m, slot], xss.at[m, j, e], xrs.at[m, slot], (src, owner * 2 + core)
        )

    def leaves(k, e):
        return 2 * e + div(rem(y + k, NY), 2) != x

    def core_sum(m, k):
        j = div(k, 2)
        for e in range(2):
            ccopy(m, k, e).wait_recv()
            xs[m, j, e] = (terms[m, k, e].astype(F32) + crecv[m, j, e].astype(F32)).astype(BF)
        for e in range(2):
            @pl.when(leaves(k, e))
            def _():
                xcopy(m, k, e).start()

    def gcopy(m):
        to = jnp.where(m == 6, rem(z + 1, NZ), plane(m))
        return rcopy(zsb.at[m], zr.at[m], gss.at[m], grs.at[m], (to * NY + y, rcv))

    def x_sum(m):
        for j in range(3):
            rcopy(xr.at[m, j], xr.at[m, j], xss.at[m, 0, 0], xrs.at[m, j], sibling).wait_recv()
        total = xs[m, div(rem(own_y + NY - y, NY), 2), own_e].astype(F32)
        for j in range(3):
            total = total + xr[m, j].astype(F32)
        zsb[m] = total.astype(BF)

        @pl.when(m == 7)
        def _():
            gcopy(jnp.int32(6)).wait_recv()
            zsb[m] = (total + zr[6].astype(F32)).astype(BF)

        @pl.when(m > 0)
        def _():
            gcopy(m).start()

    for i in range(6):
        zcopy(gx.at[i + 4], 0, i, 1).start()
        if i < 5:
            zcopy(gx.at[4 - i], 4, 4 - i, -1).start()
    ysend(jnp.int32(0), gx.at[4], gx.at[5], gx.at[3])
    zneeded(jnp.int32(1))
    zneeded(jnp.int32(2))

    load_v.wait()
    load_u.wait()

    def prepare(t, carry):
        keep = lax.broadcasted_iota(jnp.int32, (160, 256), 0) < rank_ref[0, 0, div(t, 8), rem(t, 8)]
        for c in range(2):
            part = vraw[t, :, c, :]
            v2[t, c * 160:(c + 1) * 160, :] = jnp.where(keep, part, jnp.zeros_like(part))
        ut[t] = jnp.transpose(uraw[t])
        return carry

    lax.fori_loop(0, 16, prepare, 0)
    zrest(jnp.int32(1))
    zrest(jnp.int32(2))

    def each(n, action):
        def unit(i, carry):
            k = jnp.where(i < 2, i, jnp.where(i == 2, 3, 2))
            m = jnp.where(i < 3, n, jnp.where(i == 3, n - 1, 0))
            there = jnp.where(i < 3, n < 8, jnp.where(i == 3, n > 1, n == 8))

            @pl.when(there)
            def _():
                action(m, k)

            return carry

        lax.fori_loop(0, 5, unit, 0)

    def summed(m, k):
        @pl.when(mine(k))
        def _():
            core_sum(m, k)

    def step(n, carry):
        @pl.when(jnp.logical_and(n > 0, n < 8))
        def _():
            yrelay(n)

        @pl.when(n == 7)
        def _():
            yrelay(jnp.int32(0))

        @pl.when(jnp.logical_and(n > 0, n < 6))
        def _():
            zneeded(n + 2)

        @pl.when(n > 2)
        def _():
            x_sum(n - 2)

        each(n, product)

        @pl.when(jnp.logical_and(n > 0, n < 4))
        def _():
            zrest(n + 2)

        each(n, summed)
        return carry

    lax.fori_loop(0, STEPS + 1, step, 0)
    x_sum(jnp.int32(7))
    x_sum(jnp.int32(0))

    total = zsb[0].astype(F32)
    for m in (1, 2, 3, 4, 5, 7):
        gcopy(jnp.int32(m)).wait_recv()
        total = total + zr[m].astype(F32)
    fin[...] = total.astype(BF)

    def fcopy(j):
        return rcopy(fin, fr.at[div(y, 2)], fss.at[j], frs.at[div(y, 2)], last_target(j))

    for j in range(2):
        @pl.when(jnp.logical_not(stays(j)))
        def _():
            fcopy(j).start()

        @pl.when(stays(j))
        def _():
            fr[div(y, 2)] = fin[...]

    for j in range(2):
        @pl.when(jnp.logical_not(jnp.logical_and(at_home, div(y, 2) == j)))
        def _():
            rcopy(fin, fr.at[j], fss.at[j], frs.at[j], sibling).wait_recv()

    phase = lax.bitwise_and(ws_ref[src], jnp.int32(3))
    turn = lax.bitwise_and(rem(x, 2) * 2 + lax.bitwise_and(core + phase, jnp.int32(1)) + phase, jnp.int32(3))
    chosen = jnp.where(turn < 2, fr[0], fr[1])
    fsw[...] = chosen
    swapped = rcopy(fsw, fso, sss, srs, sibling)
    swapped.start()
    swapped.wait_recv()
    result = jnp.where(lax.bitwise_and(phase, jnp.int32(1)) == 0, fsw[...], fso[...])
    out_ref[0] = result[:, 0:128]
    out_ref[1] = result[:, 128:256]
    swapped.wait_send()

    for j in range(2):
        @pl.when(jnp.logical_not(stays(j)))
        def _():
            fcopy(j).wait_send()

    for i in range(6):
        zcopy(gx.at[i + 4], 0, i, 1).wait_send()
        if i < 5:
            zcopy(gx.at[4 - i], 4, 4 - i, -1).wait_send()
    for h in range(2, 5):
        for kk in range(h - 1, 6):
            zcopy(zb.at[0, kk], h - 1, kk, 1).wait_send()
    for h in range(2, 4):
        for kk in range(0, 6 - h):
            zcopy(zb.at[0, kk], h + 3, kk, -1).wait_send()
    for k in range(1, 4):
        wcopy(k, False).wait_send()
        wcopy(k, True).wait_send()

    def drain(m, carry):
        @pl.when(jnp.logical_not(forwarded(m)))
        def _():
            for i in range(10):
                ycopy(m, i).wait_send()

        @pl.when(forwarded(m))
        def _():
            for i in (1, 2, 4, 5, 7, 9):
                ycopy(m, i, thin=True).wait_send()

        def inner(k, c):
            for e in range(2):
                @pl.when(jnp.logical_not(mine(k)))
                def _():
                    ccopy(m, k, e).wait_send()

                @pl.when(jnp.logical_and(mine(k), leaves(k, e)))
                def _():
                    xcopy(m, k, e).wait_send()

            return c

        lax.fori_loop(0, 4, inner, 0)

        @pl.when(m > 0)
        def _():
            gcopy(m).wait_send()

        return carry

    lax.fori_loop(0, STEPS, drain, 0)


def body(field, u_basis, v_basis, tile_ranks, window_start):
    fields = field.reshape(2, 8, 256, 128)
    u_tiles = u_basis.reshape(16, 320, 256)
    v_tiles = v_basis.reshape(16, 160, 2, 256)

    def blocks(*lead):
        return pltpu.VMEM((*lead, 256, 256), BF)

    def sems(*shape):
        return pltpu.SemaphoreType.DMA(shape)

    anywhere = pl.BlockSpec(memory_space=pl.ANY)
    scalars = pl.BlockSpec(memory_space=pltpu.SMEM)
    return pl.pallas_call(
        kernel,
        out_shape=jax.ShapeDtypeStruct((2, 256, 128), BF),
        in_specs=[anywhere, anywhere, anywhere, scalars, scalars],
        out_specs=pl.BlockSpec(memory_space=pltpu.VMEM),
        scratch_shapes=[
            pltpu.VMEM((2, 8, 256, 128), BF),
            blocks(10), blocks(7, 6), blocks(8, 4), blocks(8, 4), blocks(8, 3),
            pltpu.VMEM((8, 2, 128, 256), BF),
            blocks(3), blocks(8, 4, 2), blocks(8, 2, 2), blocks(8, 2, 2), blocks(8, 3), blocks(8), blocks(8),
            blocks(), blocks(2), blocks(), blocks(),
            pltpu.VMEM((16, 320, 256), BF),
            pltpu.VMEM((16, 160, 2, 256), BF),
            pltpu.VMEM((16, 256, 320), BF),
            pltpu.VMEM((16, 320, 256), BF),
            sems(3), sems(7, 6), sems(7, 6), sems(8, 10), sems(8, 10), sems(2, 3), sems(2, 3),
            sems(8, 2, 2), sems(8, 2, 2), sems(8, 2, 2), sems(8, 3), sems(8), sems(8), sems(2), sems(2),
            sems(), sems(),
        ],
        compiler_params=pltpu.CompilerParams(
            collective_id=0, has_side_effects=True, vmem_limit_bytes=60 * 1024 * 1024
        ),
    )(fields, u_tiles, v_tiles, tile_ranks, window_start)


def solution(mesh):
    return jax.shard_map(
        body,
        mesh=mesh,
        in_specs=(
            P(None, "rcv", "src"),
            P("src", "rcv", None, None, None, None, None),
            P("src", "rcv", None, None, None, None, None),
            P("src", "rcv", None, None),
            P(),
        ),
        out_specs=P(None, "rcv", "src"),
        check_vma=False,
    )
```

```python
import jax
import jax.numpy as jnp
from jax import lax
from jax.experimental import pallas as pl
from jax.experimental.pallas import tpu as pltpu
from jax.sharding import PartitionSpec as P

MESH = pl.DeviceIdType.MESH
BF = jnp.bfloat16
F32 = jnp.float32
NZ, NY, NX = 8, 4, 4
STEPS = 8


def rem(a, b):
    return lax.rem(a, jnp.int32(b))


def div(a, b):
    return lax.div(a, jnp.int32(b))


def kernel(
    field_ref, u_ref, v_ref, rank_ref, ws_ref, out_ref,
    fbuf, gx, zb, mids, oths, osend, fsend, terms, crecv, xs, xr, zsb, zr, fin, fr, fsw, fso,
    uraw, vraw, ut, v2,
    lsem, zss, zrs, yss, yrs, wss, wrs, css, crs, xss, xrs, gss, grs, fss, frs, sss, srs,
):
    src = lax.axis_index("src")
    rcv = lax.axis_index("rcv")
    z, y = div(src, NY), rem(src, NY)
    x, core = div(rcv, 2), rem(rcv, 2)
    own_y, own_e = rem(x, 2) * 2 + core, div(x, 2)
    at_home = own_y == y
    home = jnp.where(at_home, 1, 0).astype(jnp.int32)

    def zdev(offset):
        return (rem(z + (offset + 2 * NZ), NZ) * NY + y, rcv)

    def ydev(offset):
        return (z * NY + rem(y + (offset + NY), NY), rcv)

    sibling = (src, x * 2 + 1 - core)

    def rcopy(source, target, ss, rs, device):
        return pltpu.make_async_remote_copy(
            src_ref=source, dst_ref=target, send_sem=ss, recv_sem=rs,
            device_id=device, device_id_type=MESH,
        )

    load_f = pltpu.make_async_copy(field_ref, fbuf, lsem.at[0])
    load_v = pltpu.make_async_copy(v_ref, vraw, lsem.at[1])
    load_u = pltpu.make_async_copy(u_ref, uraw, lsem.at[2])
    load_f.start()

    barrier = pltpu.get_barrier_semaphore()

    def greet(device):
        pl.semaphore_signal(barrier, inc=1, device_id=device, device_id_type=MESH)

    for offset in (4, 3, 5, 2, 6, 1, 7):
        greet(zdev(offset))
    for offset in range(1, NY):
        greet(ydev(offset))
    greet(sibling)
    for offset in range(1, NX):
        greet((src, rem(x + offset, NX) * 2 + core))

    def last_target(j):
        return (z * NY + own_y, (own_e * 2 + j) * 2 + rem(y, 2))

    def stays(j):
        return jnp.logical_and(at_home, rem(x, 2) == j)

    for j in range(2):
        @pl.when(jnp.logical_not(stays(j)))
        def _():
            greet(last_target(j))

        @pl.when(jnp.logical_not(jnp.logical_and(at_home, div(y, 2) == j)))
        def _():
            greet((z * NY + core + 2 * j, (own_e * 2 + div(y, 2)) * 2 + rem(y, 2)))

    load_f.wait()
    load_v.start()
    load_u.start()
    shift = z + 19 - lax.shift_right_logical(ws_ref[src], jnp.int32(2))

    def roll_block(j, carry):
        block = lax.bitwise_and(shift + j, jnp.int32(7))
        gx[j, :, 0:128] = fbuf[0, block]
        gx[j, :, 128:256] = fbuf[1, block]
        return carry

    lax.fori_loop(0, 10, roll_block, 0)
    pl.semaphore_wait(barrier, 14 + 4 - 2 * home)

    def hop(m):
        return div(m + 1, 2) + jnp.where(m == 6, 1, 0) - jnp.where(m == 7, 1, 0)

    def plus(m):
        return rem(m + jnp.where(m > 5, 1, 0), 2) == 1

    def plane(m):
        h = hop(m)
        return rem(z + 8 + jnp.where(plus(m), -h, h), NZ)

    def forwarded(m):
        return jnp.logical_or(m == 4, m == 7)

    def zcopy(source, chain, kk, direction):
        return rcopy(source, zb.at[chain, kk], zss.at[chain, kk], zrs.at[chain, kk], zdev(direction))

    def ycopy(m, i, mid=None, thin=False):
        top, low = pl.ds(0, 128), pl.ds(128, 128)
        other = mids if thin else oths
        source, target, offset = (
            (mids.at[m, 0] if mid is None else mid, mids.at[m, 3], 1),
            (mids.at[m, 0] if mid is None else mid, mids.at[m, 1], -1),
            (osend.at[m, 0], other.at[m, 3], 1),
            (osend.at[m, 1], other.at[m, 1], -1),
            (osend.at[m, 2], other.at[m, 2], 2),
            (mids.at[m, 3, top], mids.at[m, 2, top], 1),
            (mids.at[m, 1, low], mids.at[m, 2, low], -1),
        )[i]
        return rcopy(source, target, yss.at[m, i], yrs.at[m, i], ydev(offset))

    sides = (0, 1, 3, 2)

    def phase_of(m):
        return lax.bitwise_and(ws_ref[plane(m) * NY + y], jnp.int32(3))

    def ysend(m, mid, upper, lower):
        phase = phase_of(m)

        def rows(i, carry):
            at = pl.ds(pl.multiple_of(i * 32, 32), 32)
            mids[m, 0, at] = mid[at]
            one, two = upper[at], lower[at]
            for k, target in enumerate((oths.at[m, 0], osend.at[m, 0], osend.at[m, 1], osend.at[m, 2])):
                target[at] = jnp.where(rem(y + sides[k], NY) >= phase, one, two)
            return carry

        lax.fori_loop(0, 8, rows, 0)
        for i in range(5):
            ycopy(m, i, mid).start()

    def ysend_thin(m, mid, upper, lower):
        phase = phase_of(m)

        def rows(i, carry):
            at = pl.ds(pl.multiple_of(i * 32, 32), 32)
            one, two = mid[at], lower[at]
            oths[m, 0, at] = jnp.where(y >= phase, upper[at], one)
            for k, target in enumerate((mids.at[m, 0], osend.at[m, 0], osend.at[m, 1], osend.at[m, 2])):
                target[at] = jnp.where(rem(y + sides[k], NY) >= phase, one, two)
            return carry

        lax.fori_loop(0, 8, rows, 0)
        for i in (4, 2, 3):
            ycopy(m, i, thin=True).start()

    def yrelay(m):
        @pl.when(jnp.logical_not(forwarded(m)))
        def _():
            for i in range(2):
                @pl.when(m > 0)
                def _():
                    ycopy(m, i).wait_recv()

                ycopy(m, i + 5).start()

    def zneeded(m):
        h = hop(m)

        @pl.when(plus(m))
        def _():
            chain = h - 1
            for i in range(3):
                kk = h - 1 + i
                zcopy(zb.at[chain, kk], chain, kk, 1).wait_recv()
                if i > 0:
                    @pl.when(h < 4)
                    def _():
                        zcopy(zb.at[chain, kk], chain + 1, kk, 1).start()
            ysend(m, zb.at[chain, h], zb.at[chain, h + 1], zb.at[chain, h - 1])

        @pl.when(jnp.logical_not(plus(m)))
        def _():
            chain = h + 3
            for i in range(3):
                kk = 5 - h - i
                zcopy(zb.at[chain, kk], chain, kk, -1).wait_recv()
                if i > 0:
                    @pl.when(h < 3)
                    def _():
                        zcopy(zb.at[chain, kk], chain + 1, kk, -1).start()
            blocks = zb.at[chain, 4 - h], zb.at[chain, 5 - h], zb.at[chain, 3 - h]

            @pl.when(h == 1)
            def _():
                ysend(m, *blocks)

            @pl.when(h > 1)
            def _():
                ysend_thin(m, *blocks)

    def zrest(m):
        h = hop(m)

        @pl.when(plus(m))
        def _():
            def go(kk, carry):
                zcopy(zb.at[h - 1, kk], h - 1, kk, 1).wait_recv()
                zcopy(zb.at[h - 1, kk], h, kk, 1).start()
                return carry

            lax.fori_loop(h + 2, 6, go, 0)

        @pl.when(jnp.logical_not(plus(m)))
        def _():
            def go(i, carry):
                kk = 2 - h - i
                zcopy(zb.at[h + 3, kk], h + 3, kk, -1).wait_recv()
                zcopy(zb.at[h + 3, kk], h + 4, kk, -1).start()
                return carry

            lax.fori_loop(0, 3 - h, go, 0)

    def wcopy(k, late_step):
        if late_step:
            return rcopy(mids.at[4, k], oths.at[7, k], wss.at[1, k - 1], wrs.at[1, k - 1], zdev(-1))
        return rcopy(fsend.at[k - 1], oths.at[4, k], wss.at[0, k - 1], wrs.at[0, k - 1], zdev(-1))

    def mine(k):
        return rem(y + k, 2) == core

    def ccopy(m, k, e):
        j = div(k, 2)
        return rcopy(terms.at[m, k, e], crecv.at[m, j, e], css.at[m, j, e], crs.at[m, j, e], sibling)

    def product(m, k):
        fwd = forwarded(m)

        @pl.when(jnp.logical_and(k == 1, m == 0))
        def _():
            ycopy(m, 1).wait_recv()

        @pl.when(jnp.logical_and(k == 3, m == 0))
        def _():
            ycopy(m, 0).wait_recv()

        @pl.when(k == 1)
        def _():
            ycopy(m, 3).wait_recv()

        @pl.when(k == 3)
        def _():
            ycopy(m, 2).wait_recv()

        @pl.when(k == 2)
        def _():
            ycopy(m, 4).wait_recv()

        @pl.when(jnp.logical_and(k == 2, jnp.logical_not(fwd)))
        def _():
            ycopy(m, 5).wait_recv()
            ycopy(m, 6).wait_recv()

        @pl.when(jnp.logical_and(k > 0, m == 4))
        def _():
            wcopy(k, True).start()
            wcopy(k, False).wait_recv()

        @pl.when(jnp.logical_and(k > 0, m == 7))
        def _():
            wcopy(k, True).wait_recv()

        start = ws_ref[plane(m) * NY + rem(y + k, NY)]
        phase = lax.bitwise_and(start, jnp.int32(3))
        late = jnp.where(y < phase, 1, 0).astype(jnp.int32)
        group = lax.shift_right_logical(start, jnp.int32(2)) + late
        column = lax.bitwise_and(z + 16 - group, jnp.int32(7))
        row = group * 4 + y
        tile0 = lax.shift_right_logical(row, jnp.int32(5)) * 8 + column
        tile1 = lax.shift_right_logical(row + 4, jnp.int32(5)) * 8 + lax.bitwise_and(column + 7, jnp.int32(7))
        swap = jnp.where(fwd, 0, late)

        @pl.when(jnp.logical_and(k > 0, m == 2))
        def _():
            fsend[k - 1] = jnp.where(late == 0, mids[m, k], oths[m, k])

        def item(e, inner):
            tile = jnp.where(e == 0, tile0, tile1)
            block = jnp.where(e + swap == 1, mids[m, k], oths[m, k])
            parts = jnp.dot(v2[tile], block, preferred_element_type=F32)
            w_real = (parts[:160, :128] + parts[160:, 128:]).astype(BF)
            w_imag = (parts[:160, 128:] - parts[160:, :128]).astype(BF)
            stacked = jnp.concatenate(
                [
                    jnp.concatenate([w_real, w_imag], axis=1),
                    jnp.concatenate([-w_imag, w_real], axis=1),
                ],
                axis=0,
            )
            terms[m, k, e] = jnp.dot(ut[tile], stacked, preferred_element_type=F32).astype(BF)
            return inner

        lax.fori_loop(0, 2, item, 0)

        @pl.when(jnp.logical_not(mine(k)))
        def _():
            ccopy(m, k, 0).start()
            ccopy(m, k, 1).start()

        @pl.when(jnp.logical_and(k > 0, m == 2))
        def _():
            wcopy(k, False).start()

    def xcopy(m, k, e):
        j = div(k, 2)
        owner = 2 * e + div(rem(y + k, NY), 2)
        slot = lax.max(rem(x + NX - owner, NX) - 1, jnp.int32(0))
        return rcopy(
            xs.at[m, j, e], xr.at[m, slot], xss.at[m, j, e], xrs.at[m, slot], (src, owner * 2 + core)
        )

    def leaves(k, e):
        return 2 * e + div(rem(y + k, NY), 2) != x

    def core_sum(m, k):
        j = div(k, 2)
        for e in range(2):
            ccopy(m, k, e).wait_recv()
            xs[m, j, e] = (terms[m, k, e].astype(F32) + crecv[m, j, e].astype(F32)).astype(BF)
        for e in range(2):
            @pl.when(leaves(k, e))
            def _():
                xcopy(m, k, e).start()

    def gcopy(m):
        to = jnp.where(m == 6, rem(z + 1, NZ), plane(m))
        return rcopy(zsb.at[m], zr.at[m], gss.at[m], grs.at[m], (to * NY + y, rcv))

    def x_sum(m):
        for j in range(3):
            rcopy(xr.at[m, j], xr.at[m, j], xss.at[m, 0, 0], xrs.at[m, j], sibling).wait_recv()
        total = xs[m, div(rem(own_y + NY - y, NY), 2), own_e].astype(F32)
        for j in range(3):
            total = total + xr[m, j].astype(F32)
        zsb[m] = total.astype(BF)

        @pl.when(m == 7)
        def _():
            gcopy(jnp.int32(6)).wait_recv()
            zsb[m] = (total + zr[6].astype(F32)).astype(BF)

        @pl.when(m > 0)
        def _():
            gcopy(m).start()

    for i in range(6):
        zcopy(gx.at[i + 4], 0, i, 1).start()
        if i < 5:
            zcopy(gx.at[4 - i], 4, 4 - i, -1).start()
    ysend(jnp.int32(0), gx.at[4], gx.at[5], gx.at[3])
    zneeded(jnp.int32(1))
    zneeded(jnp.int32(2))

    load_v.wait()
    load_u.wait()

    def prepare(t, carry):
        keep = lax.broadcasted_iota(jnp.int32, (160, 256), 0) < rank_ref[0, 0, div(t, 8), rem(t, 8)]
        for c in range(2):
            part = vraw[t, :, c, :]
            v2[t, c * 160:(c + 1) * 160, :] = jnp.where(keep, part, jnp.zeros_like(part))
        ut[t] = jnp.transpose(uraw[t])
        return carry

    lax.fori_loop(0, 16, prepare, 0)
    zrest(jnp.int32(1))
    zrest(jnp.int32(2))

    def each(n, action):
        def unit(i, carry):
            k = jnp.where(i < 2, i, jnp.where(i == 2, 3, 2))
            m = jnp.where(i < 3, n, jnp.where(i == 3, n - 1, 0))
            there = jnp.where(i < 3, n < 8, jnp.where(i == 3, n > 1, n == 8))

            @pl.when(there)
            def _():
                action(m, k)

            return carry

        lax.fori_loop(0, 5, unit, 0)

    def summed(m, k):
        @pl.when(mine(k))
        def _():
            core_sum(m, k)

    def step(n, carry):
        @pl.when(jnp.logical_and(n > 0, n < 8))
        def _():
            yrelay(n)

        @pl.when(n == 7)
        def _():
            yrelay(jnp.int32(0))

        @pl.when(jnp.logical_and(n > 0, n < 6))
        def _():
            zneeded(n + 2)

        each(n, product)

        @pl.when(jnp.logical_and(n > 0, n < 4))
        def _():
            zrest(n + 2)

        @pl.when(n > 2)
        def _():
            x_sum(n - 2)

        each(n, summed)
        return carry

    lax.fori_loop(0, STEPS + 1, step, 0)
    x_sum(jnp.int32(7))
    x_sum(jnp.int32(0))

    total = zsb[0].astype(F32)
    for m in (1, 2, 3, 4, 5, 7):
        gcopy(jnp.int32(m)).wait_recv()
        total = total + zr[m].astype(F32)
    fin[...] = total.astype(BF)

    def fcopy(j):
        return rcopy(fin, fr.at[div(y, 2)], fss.at[j], frs.at[div(y, 2)], last_target(j))

    for j in range(2):
        @pl.when(jnp.logical_not(stays(j)))
        def _():
            fcopy(j).start()

        @pl.when(stays(j))
        def _():
            fr[div(y, 2)] = fin[...]

    for j in range(2):
        @pl.when(jnp.logical_not(jnp.logical_and(at_home, div(y, 2) == j)))
        def _():
            rcopy(fin, fr.at[j], fss.at[j], frs.at[j], sibling).wait_recv()

    phase = lax.bitwise_and(ws_ref[src], jnp.int32(3))
    turn = lax.bitwise_and(rem(x, 2) * 2 + lax.bitwise_and(core + phase, jnp.int32(1)) + phase, jnp.int32(3))
    chosen = jnp.where(turn < 2, fr[0], fr[1])
    fsw[...] = chosen
    swapped = rcopy(fsw, fso, sss, srs, sibling)
    swapped.start()
    swapped.wait_recv()
    result = jnp.where(lax.bitwise_and(phase, jnp.int32(1)) == 0, fsw[...], fso[...])
    out_ref[0] = result[:, 0:128]
    out_ref[1] = result[:, 128:256]
    swapped.wait_send()

    for j in range(2):
        @pl.when(jnp.logical_not(stays(j)))
        def _():
            fcopy(j).wait_send()

    for i in range(6):
        zcopy(gx.at[i + 4], 0, i, 1).wait_send()
        if i < 5:
            zcopy(gx.at[4 - i], 4, 4 - i, -1).wait_send()
    for h in range(2, 5):
        for kk in range(h - 1, 6):
            zcopy(zb.at[0, kk], h - 1, kk, 1).wait_send()
    for h in range(2, 4):
        for kk in range(0, 6 - h):
            zcopy(zb.at[0, kk], h + 3, kk, -1).wait_send()
    for k in range(1, 4):
        wcopy(k, False).wait_send()
        wcopy(k, True).wait_send()

    def drain(m, carry):
        @pl.when(jnp.logical_not(forwarded(m)))
        def _():
            for i in range(7):
                ycopy(m, i).wait_send()

        @pl.when(forwarded(m))
        def _():
            for i in (2, 3, 4):
                ycopy(m, i, thin=True).wait_send()

        def inner(k, c):
            for e in range(2):
                @pl.when(jnp.logical_not(mine(k)))
                def _():
                    ccopy(m, k, e).wait_send()

                @pl.when(jnp.logical_and(mine(k), leaves(k, e)))
                def _():
                    xcopy(m, k, e).wait_send()

            return c

        lax.fori_loop(0, 4, inner, 0)

        @pl.when(m > 0)
        def _():
            gcopy(m).wait_send()

        return carry

    lax.fori_loop(0, STEPS, drain, 0)


def body(field, u_basis, v_basis, tile_ranks, window_start):
    fields = field.reshape(2, 8, 256, 128)
    u_tiles = u_basis.reshape(16, 320, 256)
    v_tiles = v_basis.reshape(16, 160, 2, 256)

    def blocks(*lead):
        return pltpu.VMEM((*lead, 256, 256), BF)

    def sems(*shape):
        return pltpu.SemaphoreType.DMA(shape)

    anywhere = pl.BlockSpec(memory_space=pl.ANY)
    scalars = pl.BlockSpec(memory_space=pltpu.SMEM)
    return pl.pallas_call(
        kernel,
        out_shape=jax.ShapeDtypeStruct((2, 256, 128), BF),
        in_specs=[anywhere, anywhere, anywhere, scalars, scalars],
        out_specs=pl.BlockSpec(memory_space=pltpu.VMEM),
        scratch_shapes=[
            pltpu.VMEM((2, 8, 256, 128), BF),
            blocks(10), blocks(7, 6), blocks(8, 4), blocks(8, 4), blocks(8, 3),
            blocks(3), blocks(8, 4, 2), blocks(8, 2, 2), blocks(8, 2, 2), blocks(8, 3), blocks(8), blocks(8),
            blocks(), blocks(2), blocks(), blocks(),
            pltpu.VMEM((16, 320, 256), BF),
            pltpu.VMEM((16, 160, 2, 256), BF),
            pltpu.VMEM((16, 256, 320), BF),
            pltpu.VMEM((16, 320, 256), BF),
            sems(3), sems(7, 6), sems(7, 6), sems(8, 7), sems(8, 7), sems(2, 3), sems(2, 3),
            sems(8, 2, 2), sems(8, 2, 2), sems(8, 2, 2), sems(8, 3), sems(8), sems(8), sems(2), sems(2),
            sems(), sems(),
        ],
        compiler_params=pltpu.CompilerParams(
            collective_id=0, has_side_effects=True, vmem_limit_bytes=60 * 1024 * 1024
        ),
    )(fields, u_tiles, v_tiles, tile_ranks, window_start)


def solution(mesh):
    return jax.shard_map(
        body,
        mesh=mesh,
        in_specs=(
            P(None, "rcv", "src"),
            P("src", "rcv", None, None, None, None, None),
            P("src", "rcv", None, None, None, None, None),
            P("src", "rcv", None, None),
            P(),
        ),
        out_specs=P(None, "rcv", "src"),
        check_vma=False,
    )
```

```python
import jax
import jax.numpy as jnp
from jax import lax
from jax.experimental import pallas as pl
from jax.experimental.pallas import tpu as pltpu
from jax.sharding import PartitionSpec as P

MESH = pl.DeviceIdType.MESH
BF = jnp.bfloat16
F32 = jnp.float32
NZ, NY, NX = 8, 4, 4
STEPS = 8


def rem(a, b):
    return lax.rem(a, jnp.int32(b))


def div(a, b):
    return lax.div(a, jnp.int32(b))


def kernel(
    field_ref, u_ref, v_ref, rank_ref, ws_ref, out_ref,
    fbuf, gx, zb, mids, oths, osend, fsend, terms, crecv, xs, xr, zsb, zr, fin, fr, fsw, fso,
    uraw, vraw, ut, v2,
    lsem, zss, zrs, yss, yrs, wss, wrs, css, crs, xss, xrs, gss, grs, fss, frs, sss, srs,
):
    src = lax.axis_index("src")
    rcv = lax.axis_index("rcv")
    z, y = div(src, NY), rem(src, NY)
    x, core = div(rcv, 2), rem(rcv, 2)
    own_y, own_e = rem(x, 2) * 2 + core, div(x, 2)
    at_home = own_y == y
    home = jnp.where(at_home, 1, 0).astype(jnp.int32)

    def zdev(offset):
        return (rem(z + (offset + 2 * NZ), NZ) * NY + y, rcv)

    def ydev(offset):
        return (z * NY + rem(y + (offset + NY), NY), rcv)

    sibling = (src, x * 2 + 1 - core)

    def rcopy(source, target, ss, rs, device):
        return pltpu.make_async_remote_copy(
            src_ref=source, dst_ref=target, send_sem=ss, recv_sem=rs,
            device_id=device, device_id_type=MESH,
        )

    load_f = pltpu.make_async_copy(field_ref, fbuf, lsem.at[0])
    load_v = pltpu.make_async_copy(v_ref, vraw, lsem.at[1])
    load_u = pltpu.make_async_copy(u_ref, uraw, lsem.at[2])
    load_f.start()

    barrier = pltpu.get_barrier_semaphore()

    def greet(device):
        pl.semaphore_signal(barrier, inc=1, device_id=device, device_id_type=MESH)

    for offset in (4, 3, 5, 2, 6, 1, 7):
        greet(zdev(offset))
    for offset in range(1, NY):
        greet(ydev(offset))
    greet(sibling)
    for offset in range(1, NX):
        greet((src, rem(x + offset, NX) * 2 + core))

    def last_target(j):
        return (z * NY + own_y, (own_e * 2 + j) * 2 + rem(y, 2))

    def stays(j):
        return jnp.logical_and(at_home, rem(x, 2) == j)

    for j in range(2):
        @pl.when(jnp.logical_not(stays(j)))
        def _():
            greet(last_target(j))

        @pl.when(jnp.logical_not(jnp.logical_and(at_home, div(y, 2) == j)))
        def _():
            greet((z * NY + core + 2 * j, (own_e * 2 + div(y, 2)) * 2 + rem(y, 2)))

    load_f.wait()
    load_v.start()
    load_u.start()
    shift = z + 19 - lax.shift_right_logical(ws_ref[src], jnp.int32(2))

    def roll_block(j, carry):
        block = lax.bitwise_and(shift + j, jnp.int32(7))
        gx[j, :, 0:128] = fbuf[0, block]
        gx[j, :, 128:256] = fbuf[1, block]
        return carry

    lax.fori_loop(0, 10, roll_block, 0)
    pl.semaphore_wait(barrier, 14 + 4 - 2 * home)

    def hop(m):
        return div(m + 1, 2) + jnp.where(m == 6, 1, 0) - jnp.where(m == 7, 1, 0)

    def plus(m):
        return rem(m + jnp.where(m > 5, 1, 0), 2) == 1

    def plane(m):
        h = hop(m)
        return rem(z + 8 + jnp.where(plus(m), -h, h), NZ)

    def forwarded(m):
        return jnp.logical_or(m == 4, m == 7)

    def zcopy(source, chain, kk, direction):
        return rcopy(source, zb.at[chain, kk], zss.at[chain, kk], zrs.at[chain, kk], zdev(direction))

    def ycopy(m, i, mid=None, thin=False):
        top, low = pl.ds(0, 128), pl.ds(128, 128)
        other = mids if thin else oths
        source, target, offset = (
            (mids.at[m, 0] if mid is None else mid, mids.at[m, 3], 1),
            (mids.at[m, 0] if mid is None else mid, mids.at[m, 1], -1),
            (osend.at[m, 0], other.at[m, 3], 1),
            (osend.at[m, 1], other.at[m, 1], -1),
            (osend.at[m, 2], other.at[m, 2], 2),
            (mids.at[m, 3, top], mids.at[m, 2, top], 1),
            (mids.at[m, 1, low], mids.at[m, 2, low], -1),
        )[i]
        return rcopy(source, target, yss.at[m, i], yrs.at[m, i], ydev(offset))

    sides = (0, 1, 3, 2)

    def phase_of(m):
        return lax.bitwise_and(ws_ref[plane(m) * NY + y], jnp.int32(3))

    def ysend(m, mid, upper, lower):
        phase = phase_of(m)

        def rows(i, carry):
            at = pl.ds(pl.multiple_of(i * 32, 32), 32)
            mids[m, 0, at] = mid[at]
            one, two = upper[at], lower[at]
            for k, target in enumerate((oths.at[m, 0], osend.at[m, 0], osend.at[m, 1], osend.at[m, 2])):
                target[at] = jnp.where(rem(y + sides[k], NY) >= phase, one, two)
            return carry

        lax.fori_loop(0, 8, rows, 0)
        for i in range(5):
            ycopy(m, i, mid).start()

    def ysend_thin(m, mid, upper, lower):
        phase = phase_of(m)

        def rows(i, carry):
            at = pl.ds(pl.multiple_of(i * 32, 32), 32)
            one, two = mid[at], lower[at]
            oths[m, 0, at] = jnp.where(y >= phase, upper[at], one)
            for k, target in enumerate((mids.at[m, 0], osend.at[m, 0], osend.at[m, 1], osend.at[m, 2])):
                target[at] = jnp.where(rem(y + sides[k], NY) >= phase, one, two)
            return carry

        lax.fori_loop(0, 8, rows, 0)
        for i in (4, 2, 3):
            ycopy(m, i, thin=True).start()

    def yrelay(m):
        @pl.when(jnp.logical_not(forwarded(m)))
        def _():
            for i in range(2):
                @pl.when(m > 0)
                def _():
                    ycopy(m, i).wait_recv()

                ycopy(m, i + 5).start()

    def zneeded(m):
        h = hop(m)

        @pl.when(plus(m))
        def _():
            chain = h - 1
            for i in range(3):
                kk = h - 1 + i
                zcopy(zb.at[chain, kk], chain, kk, 1).wait_recv()
                if i > 0:
                    @pl.when(h < 4)
                    def _():
                        zcopy(zb.at[chain, kk], chain + 1, kk, 1).start()
            ysend(m, zb.at[chain, h], zb.at[chain, h + 1], zb.at[chain, h - 1])

        @pl.when(jnp.logical_not(plus(m)))
        def _():
            chain = h + 3
            for i in range(3):
                kk = 5 - h - i
                zcopy(zb.at[chain, kk], chain, kk, -1).wait_recv()
                if i > 0:
                    @pl.when(h < 3)
                    def _():
                        zcopy(zb.at[chain, kk], chain + 1, kk, -1).start()
            blocks = zb.at[chain, 4 - h], zb.at[chain, 5 - h], zb.at[chain, 3 - h]

            @pl.when(h == 1)
            def _():
                ysend(m, *blocks)

            @pl.when(h > 1)
            def _():
                ysend_thin(m, *blocks)

    def zrest(m):
        h = hop(m)

        @pl.when(plus(m))
        def _():
            def go(kk, carry):
                zcopy(zb.at[h - 1, kk], h - 1, kk, 1).wait_recv()
                zcopy(zb.at[h - 1, kk], h, kk, 1).start()
                return carry

            lax.fori_loop(h + 2, 6, go, 0)

        @pl.when(jnp.logical_not(plus(m)))
        def _():
            def go(i, carry):
                kk = 2 - h - i
                zcopy(zb.at[h + 3, kk], h + 3, kk, -1).wait_recv()
                zcopy(zb.at[h + 3, kk], h + 4, kk, -1).start()
                return carry

            lax.fori_loop(0, 3 - h, go, 0)

    def wcopy(k, late_step):
        if late_step:
            return rcopy(mids.at[4, k], oths.at[7, k], wss.at[1, k - 1], wrs.at[1, k - 1], zdev(-1))
        return rcopy(fsend.at[k - 1], oths.at[4, k], wss.at[0, k - 1], wrs.at[0, k - 1], zdev(-1))

    def mine(k):
        return rem(y + k, 2) == core

    def ccopy(m, k, e):
        j = div(k, 2)
        return rcopy(terms.at[m, k, e], crecv.at[m, j, e], css.at[m, j, e], crs.at[m, j, e], sibling)

    def product(m, k):
        fwd = forwarded(m)

        @pl.when(jnp.logical_and(k == 1, m == 0))
        def _():
            ycopy(m, 1).wait_recv()

        @pl.when(jnp.logical_and(k == 3, m == 0))
        def _():
            ycopy(m, 0).wait_recv()

        @pl.when(k == 1)
        def _():
            ycopy(m, 3).wait_recv()

        @pl.when(k == 3)
        def _():
            ycopy(m, 2).wait_recv()

        @pl.when(k == 2)
        def _():
            ycopy(m, 4).wait_recv()

        @pl.when(jnp.logical_and(k == 2, jnp.logical_not(fwd)))
        def _():
            ycopy(m, 5).wait_recv()
            ycopy(m, 6).wait_recv()

        @pl.when(jnp.logical_and(k > 0, m == 4))
        def _():
            wcopy(k, True).start()
            wcopy(k, False).wait_recv()

        @pl.when(jnp.logical_and(k > 0, m == 7))
        def _():
            wcopy(k, True).wait_recv()

        start = ws_ref[plane(m) * NY + rem(y + k, NY)]
        phase = lax.bitwise_and(start, jnp.int32(3))
        late = jnp.where(y < phase, 1, 0).astype(jnp.int32)
        group = lax.shift_right_logical(start, jnp.int32(2)) + late
        column = lax.bitwise_and(z + 16 - group, jnp.int32(7))
        row = group * 4 + y
        tile0 = lax.shift_right_logical(row, jnp.int32(5)) * 8 + column
        tile1 = lax.shift_right_logical(row + 4, jnp.int32(5)) * 8 + lax.bitwise_and(column + 7, jnp.int32(7))
        swap = jnp.where(fwd, 0, late)

        @pl.when(jnp.logical_and(k > 0, m == 2))
        def _():
            fsend[k - 1] = jnp.where(late == 0, mids[m, k], oths[m, k])

        def item(e, inner):
            tile = jnp.where(e == 0, tile0, tile1)
            block = jnp.where(e + swap == 1, mids[m, k], oths[m, k])
            parts = jnp.dot(v2[tile], block, preferred_element_type=F32)
            w_real = (parts[:160, :128] + parts[160:, 128:]).astype(BF)
            w_imag = (parts[:160, 128:] - parts[160:, :128]).astype(BF)
            stacked = jnp.concatenate(
                [
                    jnp.concatenate([w_real, w_imag], axis=1),
                    jnp.concatenate([-w_imag, w_real], axis=1),
                ],
                axis=0,
            )
            terms[m, k, e] = jnp.dot(ut[tile], stacked, preferred_element_type=F32).astype(BF)
            return inner

        lax.fori_loop(0, 2, item, 0)

        @pl.when(jnp.logical_not(mine(k)))
        def _():
            ccopy(m, k, 0).start()
            ccopy(m, k, 1).start()

        @pl.when(jnp.logical_and(k > 0, m == 2))
        def _():
            wcopy(k, False).start()

    def xcopy(m, k, e):
        j = div(k, 2)
        owner = 2 * e + div(rem(y + k, NY), 2)
        slot = lax.max(rem(x + NX - owner, NX) - 1, jnp.int32(0))
        return rcopy(
            xs.at[m, j, e], xr.at[m, slot], xss.at[m, j, e], xrs.at[m, slot], (src, owner * 2 + core)
        )

    def leaves(k, e):
        return 2 * e + div(rem(y + k, NY), 2) != x

    def core_sum(m, k):
        j = div(k, 2)
        for e in range(2):
            ccopy(m, k, e).wait_recv()
            xs[m, j, e] = (terms[m, k, e].astype(F32) + crecv[m, j, e].astype(F32)).astype(BF)
        for e in range(2):
            @pl.when(leaves(k, e))
            def _():
                xcopy(m, k, e).start()

    def gcopy(m):
        to = jnp.where(m == 6, rem(z + 1, NZ), plane(m))
        return rcopy(zsb.at[m], zr.at[m], gss.at[m], grs.at[m], (to * NY + y, rcv))

    def x_sum(m):
        for j in range(3):
            rcopy(xr.at[m, j], xr.at[m, j], xss.at[m, 0, 0], xrs.at[m, j], sibling).wait_recv()
        total = xs[m, div(rem(own_y + NY - y, NY), 2), own_e].astype(F32)
        for j in range(3):
            total = total + xr[m, j].astype(F32)
        zsb[m] = total.astype(BF)

        @pl.when(m == 7)
        def _():
            gcopy(jnp.int32(6)).wait_recv()
            zsb[m] = (total + zr[6].astype(F32)).astype(BF)

        @pl.when(m > 0)
        def _():
            gcopy(m).start()

    for i in range(6):
        zcopy(gx.at[i + 4], 0, i, 1).start()
        if i < 5:
            zcopy(gx.at[4 - i], 4, 4 - i, -1).start()
    ysend(jnp.int32(0), gx.at[4], gx.at[5], gx.at[3])
    zneeded(jnp.int32(1))
    zneeded(jnp.int32(2))

    load_v.wait()
    load_u.wait()

    def prepare(t, carry):
        keep = lax.broadcasted_iota(jnp.int32, (160, 256), 0) < rank_ref[0, 0, div(t, 8), rem(t, 8)]
        for c in range(2):
            part = vraw[t, :, c, :]
            v2[t, c * 160:(c + 1) * 160, :] = jnp.where(keep, part, jnp.zeros_like(part))
        ut[t] = jnp.transpose(uraw[t])
        return carry

    lax.fori_loop(0, 16, prepare, 0)
    zrest(jnp.int32(1))
    zrest(jnp.int32(2))

    def each(n, action):
        def unit(i, carry):
            k = jnp.where(i < 2, i, jnp.where(i == 2, 3, 2))
            m = jnp.where(i < 3, n, jnp.where(i == 3, n - 1, 0))
            there = jnp.where(i < 3, n < 8, jnp.where(i == 3, n > 1, n == 8))

            @pl.when(there)
            def _():
                action(m, k)

            return carry

        lax.fori_loop(0, 5, unit, 0)

    def summed(m, k):
        @pl.when(mine(k))
        def _():
            core_sum(m, k)

    def step(n, carry):
        @pl.when(jnp.logical_and(n > 0, n < 8))
        def _():
            yrelay(n)

        @pl.when(n == 7)
        def _():
            yrelay(jnp.int32(0))

        @pl.when(jnp.logical_and(n > 0, n < 6))
        def _():
            zneeded(n + 2)

        each(n, product)

        @pl.when(jnp.logical_and(n > 0, n < 4))
        def _():
            zrest(n + 2)

        @pl.when(n > 2)
        def _():
            x_sum(n - 2)

        each(n, summed)
        return carry

    lax.fori_loop(0, STEPS + 1, step, 0)
    x_sum(jnp.int32(7))
    x_sum(jnp.int32(0))

    for i in range(6):
        zcopy(gx.at[i + 4], 0, i, 1).wait_send()
        if i < 5:
            zcopy(gx.at[4 - i], 4, 4 - i, -1).wait_send()
    for h in range(2, 5):
        for kk in range(h - 1, 6):
            zcopy(zb.at[0, kk], h - 1, kk, 1).wait_send()
    for h in range(2, 4):
        for kk in range(0, 6 - h):
            zcopy(zb.at[0, kk], h + 3, kk, -1).wait_send()
    for k in range(1, 4):
        wcopy(k, False).wait_send()
        wcopy(k, True).wait_send()

    def drain(m, carry):
        @pl.when(jnp.logical_not(forwarded(m)))
        def _():
            for i in range(7):
                ycopy(m, i).wait_send()

        @pl.when(forwarded(m))
        def _():
            for i in (2, 3, 4):
                ycopy(m, i, thin=True).wait_send()

        def inner(k, c):
            for e in range(2):
                @pl.when(jnp.logical_not(mine(k)))
                def _():
                    ccopy(m, k, e).wait_send()

                @pl.when(jnp.logical_and(mine(k), leaves(k, e)))
                def _():
                    xcopy(m, k, e).wait_send()

            return c

        lax.fori_loop(0, 4, inner, 0)

        return carry

    lax.fori_loop(0, STEPS, drain, 0)

    total = zsb[0].astype(F32)
    for m in (1, 2, 3, 4, 5, 7):
        gcopy(jnp.int32(m)).wait_recv()
        total = total + zr[m].astype(F32)
    fin[...] = total.astype(BF)

    def fcopy(j):
        return rcopy(fin, fr.at[div(y, 2)], fss.at[j], frs.at[div(y, 2)], last_target(j))

    for j in range(2):
        @pl.when(jnp.logical_not(stays(j)))
        def _():
            fcopy(j).start()

        @pl.when(stays(j))
        def _():
            fr[div(y, 2)] = fin[...]

    for j in range(2):
        @pl.when(jnp.logical_not(jnp.logical_and(at_home, div(y, 2) == j)))
        def _():
            rcopy(fin, fr.at[j], fss.at[j], frs.at[j], sibling).wait_recv()

    phase = lax.bitwise_and(ws_ref[src], jnp.int32(3))
    turn = lax.bitwise_and(rem(x, 2) * 2 + lax.bitwise_and(core + phase, jnp.int32(1)) + phase, jnp.int32(3))
    chosen = jnp.where(turn < 2, fr[0], fr[1])
    fsw[...] = chosen
    swapped = rcopy(fsw, fso, sss, srs, sibling)
    swapped.start()
    swapped.wait_recv()
    result = jnp.where(lax.bitwise_and(phase, jnp.int32(1)) == 0, fsw[...], fso[...])
    out_ref[0] = result[:, 0:128]
    out_ref[1] = result[:, 128:256]
    swapped.wait_send()

    for j in range(2):
        @pl.when(jnp.logical_not(stays(j)))
        def _():
            fcopy(j).wait_send()

    for m in range(1, STEPS):
        gcopy(jnp.int32(m)).wait_send()


def body(field, u_basis, v_basis, tile_ranks, window_start):
    fields = field.reshape(2, 8, 256, 128)
    u_tiles = u_basis.reshape(16, 320, 256)
    v_tiles = v_basis.reshape(16, 160, 2, 256)

    def blocks(*lead):
        return pltpu.VMEM((*lead, 256, 256), BF)

    def sems(*shape):
        return pltpu.SemaphoreType.DMA(shape)

    anywhere = pl.BlockSpec(memory_space=pl.ANY)
    scalars = pl.BlockSpec(memory_space=pltpu.SMEM)
    return pl.pallas_call(
        kernel,
        out_shape=jax.ShapeDtypeStruct((2, 256, 128), BF),
        in_specs=[anywhere, anywhere, anywhere, scalars, scalars],
        out_specs=pl.BlockSpec(memory_space=pltpu.VMEM),
        scratch_shapes=[
            pltpu.VMEM((2, 8, 256, 128), BF),
            blocks(10), blocks(7, 6), blocks(8, 4), blocks(8, 4), blocks(8, 3),
            blocks(3), blocks(8, 4, 2), blocks(8, 2, 2), blocks(8, 2, 2), blocks(8, 3), blocks(8), blocks(8),
            blocks(), blocks(2), blocks(), blocks(),
            pltpu.VMEM((16, 320, 256), BF),
            pltpu.VMEM((16, 160, 2, 256), BF),
            pltpu.VMEM((16, 256, 320), BF),
            pltpu.VMEM((16, 320, 256), BF),
            sems(3), sems(7, 6), sems(7, 6), sems(8, 7), sems(8, 7), sems(2, 3), sems(2, 3),
            sems(8, 2, 2), sems(8, 2, 2), sems(8, 2, 2), sems(8, 3), sems(8), sems(8), sems(2), sems(2),
            sems(), sems(),
        ],
        compiler_params=pltpu.CompilerParams(
            collective_id=0, has_side_effects=True, vmem_limit_bytes=60 * 1024 * 1024
        ),
    )(fields, u_tiles, v_tiles, tile_ranks, window_start)


def solution(mesh):
    return jax.shard_map(
        body,
        mesh=mesh,
        in_specs=(
            P(None, "rcv", "src"),
            P("src", "rcv", None, None, None, None, None),
            P("src", "rcv", None, None, None, None, None),
            P("src", "rcv", None, None),
            P(),
        ),
        out_specs=P(None, "rcv", "src"),
        check_vma=False,
    )
```

```python
import jax
import jax.numpy as jnp
from jax import lax
from jax.experimental import pallas as pl
from jax.experimental.pallas import tpu as pltpu
from jax.sharding import PartitionSpec as P

MESH = pl.DeviceIdType.MESH
BF = jnp.bfloat16
F32 = jnp.float32
NZ, NY, NX = 8, 4, 4
STEPS = 8


def rem(a, b):
    return lax.rem(a, jnp.int32(b))


def div(a, b):
    return lax.div(a, jnp.int32(b))


def kernel(
    field_ref, u_ref, v_ref, rank_ref, ws_ref, out_ref,
    fbuf, gx, zb, mids, oths, osend, fsend, terms, crecv, xs, xr, zsb, zr, fin, fr, fsw, fso,
    uraw, vraw, ut, v2,
    lsem, zss, zrs, yss, yrs, wss, wrs, css, crs, xss, xrs, gss, grs, fss, frs, sss, srs,
):
    src = lax.axis_index("src")
    rcv = lax.axis_index("rcv")
    z, y = div(src, NY), rem(src, NY)
    x, core = div(rcv, 2), rem(rcv, 2)
    own_y, own_e = rem(x, 2) * 2 + core, div(x, 2)
    at_home = own_y == y
    home = jnp.where(at_home, 1, 0).astype(jnp.int32)

    def zdev(offset):
        return (rem(z + (offset + 2 * NZ), NZ) * NY + y, rcv)

    def ydev(offset):
        return (z * NY + rem(y + (offset + NY), NY), rcv)

    sibling = (src, x * 2 + 1 - core)

    def rcopy(source, target, ss, rs, device):
        return pltpu.make_async_remote_copy(
            src_ref=source, dst_ref=target, send_sem=ss, recv_sem=rs,
            device_id=device, device_id_type=MESH,
        )

    load_f = pltpu.make_async_copy(field_ref, fbuf, lsem.at[0])
    load_v = pltpu.make_async_copy(v_ref, vraw, lsem.at[1])
    load_u = pltpu.make_async_copy(u_ref, uraw, lsem.at[2])
    load_f.start()

    barrier = pltpu.get_barrier_semaphore()

    def greet(device):
        pl.semaphore_signal(barrier, inc=1, device_id=device, device_id_type=MESH)

    for offset in (4, 3, 5, 2, 6, 1, 7):
        greet(zdev(offset))
    for offset in range(1, NY):
        greet(ydev(offset))
    greet(sibling)
    for offset in range(1, NX):
        greet((src, rem(x + offset, NX) * 2 + core))

    def last_target(j):
        return (z * NY + own_y, (own_e * 2 + j) * 2 + rem(y, 2))

    def stays(j):
        return jnp.logical_and(at_home, rem(x, 2) == j)

    for j in range(2):
        @pl.when(jnp.logical_not(stays(j)))
        def _():
            greet(last_target(j))

        @pl.when(jnp.logical_not(jnp.logical_and(at_home, div(y, 2) == j)))
        def _():
            greet((z * NY + core + 2 * j, (own_e * 2 + div(y, 2)) * 2 + rem(y, 2)))

    load_f.wait()
    load_v.start()
    load_u.start()
    shift = z + 19 - lax.shift_right_logical(ws_ref[src], jnp.int32(2))

    def roll_block(j, carry):
        block = lax.bitwise_and(shift + j, jnp.int32(7))
        gx[j, :, 0:128] = fbuf[0, block]
        gx[j, :, 128:256] = fbuf[1, block]
        return carry

    lax.fori_loop(0, 10, roll_block, 0)
    pl.semaphore_wait(barrier, 14 + 4 - 2 * home)

    def hop(m):
        return div(m + 1, 2) + jnp.where(m == 6, 1, 0) - jnp.where(m == 7, 1, 0)

    def plus(m):
        return rem(m + jnp.where(m > 5, 1, 0), 2) == 1

    def plane(m):
        h = hop(m)
        return rem(z + 8 + jnp.where(plus(m), -h, h), NZ)

    def forwarded(m):
        return jnp.logical_or(m == 4, m == 7)

    def zcopy(source, chain, kk, direction):
        return rcopy(source, zb.at[chain, kk], zss.at[chain, kk], zrs.at[chain, kk], zdev(direction))

    def ycopy(m, i, mid=None, thin=False):
        top, low = pl.ds(0, 128), pl.ds(128, 128)
        other = mids if thin else oths
        source, target, offset = (
            (mids.at[m, 0] if mid is None else mid, mids.at[m, 3], 1),
            (mids.at[m, 0] if mid is None else mid, mids.at[m, 1], -1),
            (osend.at[m, 0], other.at[m, 3], 1),
            (osend.at[m, 1], other.at[m, 1], -1),
            (osend.at[m, 2], other.at[m, 2], 2),
            (mids.at[m, 3, top], mids.at[m, 2, top], 1),
            (mids.at[m, 1, low], mids.at[m, 2, low], -1),
        )[i]
        return rcopy(source, target, yss.at[m, i], yrs.at[m, i], ydev(offset))

    sides = (0, 1, 3, 2)

    def phase_of(m):
        return lax.bitwise_and(ws_ref[plane(m) * NY + y], jnp.int32(3))

    def ysend(m, mid, upper, lower):
        phase = phase_of(m)

        def rows(i, carry):
            at = pl.ds(pl.multiple_of(i * 32, 32), 32)
            mids[m, 0, at] = mid[at]
            one, two = upper[at], lower[at]
            for k, target in enumerate((oths.at[m, 0], osend.at[m, 0], osend.at[m, 1], osend.at[m, 2])):
                target[at] = jnp.where(rem(y + sides[k], NY) >= phase, one, two)
            return carry

        lax.fori_loop(0, 8, rows, 0)
        for i in range(5):
            ycopy(m, i, mid).start()

    def ysend_thin(m, mid, upper, lower):
        phase = phase_of(m)

        def rows(i, carry):
            at = pl.ds(pl.multiple_of(i * 32, 32), 32)
            one, two = mid[at], lower[at]
            oths[m, 0, at] = jnp.where(y >= phase, upper[at], one)
            for k, target in enumerate((mids.at[m, 0], osend.at[m, 0], osend.at[m, 1], osend.at[m, 2])):
                target[at] = jnp.where(rem(y + sides[k], NY) >= phase, one, two)
            return carry

        lax.fori_loop(0, 8, rows, 0)
        for i in (4, 2, 3):
            ycopy(m, i, thin=True).start()

    def yrelay(m):
        @pl.when(jnp.logical_not(forwarded(m)))
        def _():
            for i in range(2):
                @pl.when(m > 0)
                def _():
                    ycopy(m, i).wait_recv()

                ycopy(m, i + 5).start()

    def zneeded(m):
        h = hop(m)

        @pl.when(plus(m))
        def _():
            chain = h - 1
            for i in range(3):
                kk = h - 1 + i
                zcopy(zb.at[chain, kk], chain, kk, 1).wait_recv()
                if i > 0:
                    @pl.when(h < 4)
                    def _():
                        zcopy(zb.at[chain, kk], chain + 1, kk, 1).start()
            ysend(m, zb.at[chain, h], zb.at[chain, h + 1], zb.at[chain, h - 1])

        @pl.when(jnp.logical_not(plus(m)))
        def _():
            chain = h + 3
            for i in range(3):
                kk = 5 - h - i
                zcopy(zb.at[chain, kk], chain, kk, -1).wait_recv()
                if i > 0:
                    @pl.when(h < 3)
                    def _():
                        zcopy(zb.at[chain, kk], chain + 1, kk, -1).start()
            blocks = zb.at[chain, 4 - h], zb.at[chain, 5 - h], zb.at[chain, 3 - h]

            @pl.when(h == 1)
            def _():
                ysend(m, *blocks)

            @pl.when(h > 1)
            def _():
                ysend_thin(m, *blocks)

    def zrest(m):
        h = hop(m)

        @pl.when(plus(m))
        def _():
            def go(kk, carry):
                zcopy(zb.at[h - 1, kk], h - 1, kk, 1).wait_recv()
                zcopy(zb.at[h - 1, kk], h, kk, 1).start()
                return carry

            lax.fori_loop(h + 2, 6, go, 0)

        @pl.when(jnp.logical_not(plus(m)))
        def _():
            def go(i, carry):
                kk = 2 - h - i
                zcopy(zb.at[h + 3, kk], h + 3, kk, -1).wait_recv()
                zcopy(zb.at[h + 3, kk], h + 4, kk, -1).start()
                return carry

            lax.fori_loop(0, 3 - h, go, 0)

    def wcopy(k, late_step):
        if late_step:
            return rcopy(mids.at[4, k], oths.at[7, k], wss.at[1, k - 1], wrs.at[1, k - 1], zdev(-1))
        return rcopy(fsend.at[k - 1], oths.at[4, k], wss.at[0, k - 1], wrs.at[0, k - 1], zdev(-1))

    def mine(k):
        return rem(y + k, 2) == core

    def ccopy(m, k, e):
        j = div(k, 2)
        return rcopy(terms.at[m, k, e], crecv.at[m, j, e], css.at[m, j, e], crs.at[m, j, e], sibling)

    def product(m, k):
        fwd = forwarded(m)

        @pl.when(jnp.logical_and(k == 1, m == 0))
        def _():
            ycopy(m, 1).wait_recv()

        @pl.when(jnp.logical_and(k == 3, m == 0))
        def _():
            ycopy(m, 0).wait_recv()

        @pl.when(k == 1)
        def _():
            ycopy(m, 3).wait_recv()

        @pl.when(k == 3)
        def _():
            ycopy(m, 2).wait_recv()

        @pl.when(k == 2)
        def _():
            ycopy(m, 4).wait_recv()

        @pl.when(jnp.logical_and(k == 2, jnp.logical_not(fwd)))
        def _():
            ycopy(m, 5).wait_recv()
            ycopy(m, 6).wait_recv()

        @pl.when(jnp.logical_and(k > 0, m == 4))
        def _():
            wcopy(k, True).start()
            wcopy(k, False).wait_recv()

        @pl.when(jnp.logical_and(k > 0, m == 7))
        def _():
            wcopy(k, True).wait_recv()

        start = ws_ref[plane(m) * NY + rem(y + k, NY)]
        phase = lax.bitwise_and(start, jnp.int32(3))
        late = jnp.where(y < phase, 1, 0).astype(jnp.int32)
        group = lax.shift_right_logical(start, jnp.int32(2)) + late
        column = lax.bitwise_and(z + 16 - group, jnp.int32(7))
        row = group * 4 + y
        tile0 = lax.shift_right_logical(row, jnp.int32(5)) * 8 + column
        tile1 = lax.shift_right_logical(row + 4, jnp.int32(5)) * 8 + lax.bitwise_and(column + 7, jnp.int32(7))
        swap = jnp.where(fwd, 0, late)

        @pl.when(jnp.logical_and(k > 0, m == 2))
        def _():
            fsend[k - 1] = jnp.where(late == 0, mids[m, k], oths[m, k])

        def item(e, inner):
            tile = jnp.where(e == 0, tile0, tile1)
            block = jnp.where(e + swap == 1, mids[m, k], oths[m, k])
            parts = jnp.dot(v2[tile], block, preferred_element_type=F32)
            w_real = (parts[:160, :128] + parts[160:, 128:]).astype(BF)
            w_imag = (parts[:160, 128:] - parts[160:, :128]).astype(BF)
            stacked = jnp.concatenate(
                [
                    jnp.concatenate([w_real, w_imag], axis=1),
                    jnp.concatenate([-w_imag, w_real], axis=1),
                ],
                axis=0,
            )
            terms[m, k, e] = jnp.dot(ut[tile], stacked, preferred_element_type=F32).astype(BF)
            return inner

        lax.fori_loop(0, 2, item, 0)

        @pl.when(jnp.logical_not(mine(k)))
        def _():
            ccopy(m, k, 0).start()
            ccopy(m, k, 1).start()

        @pl.when(jnp.logical_and(k > 0, m == 2))
        def _():
            wcopy(k, False).start()

    def xcopy(m, k, e):
        j = div(k, 2)
        owner = 2 * e + div(rem(y + k, NY), 2)
        slot = lax.max(rem(x + NX - owner, NX) - 1, jnp.int32(0))
        return rcopy(
            xs.at[m, j, e], xr.at[m, slot], xss.at[m, j, e], xrs.at[m, slot], (src, owner * 2 + core)
        )

    def leaves(k, e):
        return 2 * e + div(rem(y + k, NY), 2) != x

    def core_sum(m, k):
        j = div(k, 2)
        for e in range(2):
            ccopy(m, k, e).wait_recv()
            xs[m, j, e] = (terms[m, k, e].astype(F32) + crecv[m, j, e].astype(F32)).astype(BF)
        for e in range(2):
            @pl.when(leaves(k, e))
            def _():
                xcopy(m, k, e).start()

    def gcopy(m):
        to = plane(m)
        return rcopy(zsb.at[m], zr.at[m], gss.at[m], grs.at[m], (to * NY + y, rcv))

    def x_sum(m):
        for j in range(3):
            rcopy(xr.at[m, j], xr.at[m, j], xss.at[m, 0, 0], xrs.at[m, j], sibling).wait_recv()
        total = xs[m, div(rem(own_y + NY - y, NY), 2), own_e].astype(F32)
        for j in range(3):
            total = total + xr[m, j].astype(F32)
        zsb[m] = total.astype(BF)

        @pl.when(m > 0)
        def _():
            gcopy(m).start()

    for i in range(6):
        zcopy(gx.at[i + 4], 0, i, 1).start()
        if i < 5:
            zcopy(gx.at[4 - i], 4, 4 - i, -1).start()
    ysend(jnp.int32(0), gx.at[4], gx.at[5], gx.at[3])
    zneeded(jnp.int32(1))
    zneeded(jnp.int32(2))

    load_v.wait()
    load_u.wait()

    def prepare(t, carry):
        keep = lax.broadcasted_iota(jnp.int32, (160, 256), 0) < rank_ref[0, 0, div(t, 8), rem(t, 8)]
        for c in range(2):
            part = vraw[t, :, c, :]
            v2[t, c * 160:(c + 1) * 160, :] = jnp.where(keep, part, jnp.zeros_like(part))
        ut[t] = jnp.transpose(uraw[t])
        return carry

    lax.fori_loop(0, 16, prepare, 0)
    zrest(jnp.int32(1))
    zrest(jnp.int32(2))

    def each(n, action):
        def unit(i, carry):
            k = jnp.where(i < 2, i, jnp.where(i == 2, 3, 2))
            m = jnp.where(i < 3, n, jnp.where(i == 3, n - 1, 0))
            there = jnp.where(i < 3, n < 8, jnp.where(i == 3, n > 1, n == 8))

            @pl.when(there)
            def _():
                action(m, k)

            return carry

        lax.fori_loop(0, 5, unit, 0)

    def summed(m, k):
        @pl.when(mine(k))
        def _():
            core_sum(m, k)

    def step(n, carry):
        @pl.when(jnp.logical_and(n > 0, n < 8))
        def _():
            yrelay(n)

        @pl.when(n == 7)
        def _():
            yrelay(jnp.int32(0))

        @pl.when(jnp.logical_and(n > 0, n < 6))
        def _():
            zneeded(n + 2)

        each(n, product)

        @pl.when(jnp.logical_and(n > 0, n < 4))
        def _():
            zrest(n + 2)

        @pl.when(n > 2)
        def _():
            x_sum(n - 2)

        each(n, summed)
        return carry

    lax.fori_loop(0, STEPS + 1, step, 0)
    x_sum(jnp.int32(7))
    x_sum(jnp.int32(0))

    for i in range(6):
        zcopy(gx.at[i + 4], 0, i, 1).wait_send()
        if i < 5:
            zcopy(gx.at[4 - i], 4, 4 - i, -1).wait_send()
    for h in range(2, 5):
        for kk in range(h - 1, 6):
            zcopy(zb.at[0, kk], h - 1, kk, 1).wait_send()
    for h in range(2, 4):
        for kk in range(0, 6 - h):
            zcopy(zb.at[0, kk], h + 3, kk, -1).wait_send()
    for k in range(1, 4):
        wcopy(k, False).wait_send()
        wcopy(k, True).wait_send()

    def drain(m, carry):
        @pl.when(jnp.logical_not(forwarded(m)))
        def _():
            for i in range(7):
                ycopy(m, i).wait_send()

        @pl.when(forwarded(m))
        def _():
            for i in (2, 3, 4):
                ycopy(m, i, thin=True).wait_send()

        def inner(k, c):
            for e in range(2):
                @pl.when(jnp.logical_not(mine(k)))
                def _():
                    ccopy(m, k, e).wait_send()

                @pl.when(jnp.logical_and(mine(k), leaves(k, e)))
                def _():
                    xcopy(m, k, e).wait_send()

            return c

        lax.fori_loop(0, 4, inner, 0)

        return carry

    lax.fori_loop(0, STEPS, drain, 0)

    total = zsb[0].astype(F32)
    for m in range(1, STEPS):
        gcopy(jnp.int32(m)).wait_recv()
        total = total + zr[m].astype(F32)
    fin[...] = total.astype(BF)

    def fcopy(j):
        return rcopy(fin, fr.at[div(y, 2)], fss.at[j], frs.at[div(y, 2)], last_target(j))

    for j in range(2):
        @pl.when(jnp.logical_not(stays(j)))
        def _():
            fcopy(j).start()

        @pl.when(stays(j))
        def _():
            fr[div(y, 2)] = fin[...]

    for j in range(2):
        @pl.when(jnp.logical_not(jnp.logical_and(at_home, div(y, 2) == j)))
        def _():
            rcopy(fin, fr.at[j], fss.at[j], frs.at[j], sibling).wait_recv()

    phase = lax.bitwise_and(ws_ref[src], jnp.int32(3))
    turn = lax.bitwise_and(rem(x, 2) * 2 + lax.bitwise_and(core + phase, jnp.int32(1)) + phase, jnp.int32(3))
    chosen = jnp.where(turn < 2, fr[0], fr[1])
    fsw[...] = chosen
    swapped = rcopy(fsw, fso, sss, srs, sibling)
    swapped.start()
    swapped.wait_recv()
    result = jnp.where(lax.bitwise_and(phase, jnp.int32(1)) == 0, fsw[...], fso[...])
    out_ref[0] = result[:, 0:128]
    out_ref[1] = result[:, 128:256]
    swapped.wait_send()

    for j in range(2):
        @pl.when(jnp.logical_not(stays(j)))
        def _():
            fcopy(j).wait_send()

    for m in range(1, STEPS):
        gcopy(jnp.int32(m)).wait_send()


def body(field, u_basis, v_basis, tile_ranks, window_start):
    fields = field.reshape(2, 8, 256, 128)
    u_tiles = u_basis.reshape(16, 320, 256)
    v_tiles = v_basis.reshape(16, 160, 2, 256)

    def blocks(*lead):
        return pltpu.VMEM((*lead, 256, 256), BF)

    def sems(*shape):
        return pltpu.SemaphoreType.DMA(shape)

    anywhere = pl.BlockSpec(memory_space=pl.ANY)
    scalars = pl.BlockSpec(memory_space=pltpu.SMEM)
    return pl.pallas_call(
        kernel,
        out_shape=jax.ShapeDtypeStruct((2, 256, 128), BF),
        in_specs=[anywhere, anywhere, anywhere, scalars, scalars],
        out_specs=pl.BlockSpec(memory_space=pltpu.VMEM),
        scratch_shapes=[
            pltpu.VMEM((2, 8, 256, 128), BF),
            blocks(10), blocks(7, 6), blocks(8, 4), blocks(8, 4), blocks(8, 3),
            blocks(3), blocks(8, 4, 2), blocks(8, 2, 2), blocks(8, 2, 2), blocks(8, 3), blocks(8), blocks(8),
            blocks(), blocks(2), blocks(), blocks(),
            pltpu.VMEM((16, 320, 256), BF),
            pltpu.VMEM((16, 160, 2, 256), BF),
            pltpu.VMEM((16, 256, 320), BF),
            pltpu.VMEM((16, 320, 256), BF),
            sems(3), sems(7, 6), sems(7, 6), sems(8, 7), sems(8, 7), sems(2, 3), sems(2, 3),
            sems(8, 2, 2), sems(8, 2, 2), sems(8, 2, 2), sems(8, 3), sems(8), sems(8), sems(2), sems(2),
            sems(), sems(),
        ],
        compiler_params=pltpu.CompilerParams(
            collective_id=0, has_side_effects=True, vmem_limit_bytes=60 * 1024 * 1024
        ),
    )(fields, u_tiles, v_tiles, tile_ranks, window_start)


def solution(mesh):
    return jax.shard_map(
        body,
        mesh=mesh,
        in_specs=(
            P(None, "rcv", "src"),
            P("src", "rcv", None, None, None, None, None),
            P("src", "rcv", None, None, None, None, None),
            P("src", "rcv", None, None),
            P(),
        ),
        out_specs=P(None, "rcv", "src"),
        check_vma=False,
    )
```
